32 devices in a mesh: pair: 4 (over y, x), mat: 8 (over z, core).
Axes of the slice: x: 2, y: 2, z: 4, core: 2. Of those that a mesh axis runs over, the one named last changes fastest.
Arguments:
- operators: bfloat16 [16, 2048, 2048], P('pair', 'mat'), may hold values from -6 to 6
- left_rot: bfloat16 [2048, 2048], P('mat'), may hold values from -0.125 to 0.125
- right_rot: bfloat16 [2048, 2048], P('mat'), may hold values from -0.125 to 0.125
- integrals: float32 [1024, 1024], replicated, may hold values from -1.5 to 1.5
- pair_index: int32 [16], replicated, may hold values from 0 to 1023
- target_index: int32 [16], replicated, may hold values from 0 to 1023
Outputs:
- complement: bfloat16 [16, 2048, 2048], P('pair', None, 'mat')
The draws below stay inside these ranges and needn't reach their ends.
All inputs are finite; a program needn't handle non-finite values.
Results may differ from the reference program's by a relative error of at most 0.0063.
Values may be sent and summed in bfloat16 or wider, within the bound.
A program may use at most 192 MiB of HBM per device.

```python
import jax
import jax.numpy as jnp
from jax import lax

M = 2048
NPQ = 1024
NSEL = 16
NTGT = 16


def set_ends(values, key, least, high):
    shape = values.shape
    spot = [jax.random.randint(jax.random.fold_in(key, axis), (), 0, shape[axis]) for axis in range(len(shape))]
    values = values.at[tuple(spot)].set(least)
    longest = shape.index(max(shape))
    spot[longest] = (spot[longest] + 1) % shape[longest]
    return values.at[tuple(spot)].set(high)


def shard_levels(stream_key, dims, shards, least, high):
    gain = 1.0
    for position, shards_of in shards:
        heights = jax.random.uniform(jax.random.fold_in(jax.random.fold_in(stream_key, 6), position), (shards_of,), jnp.float32, least / len(shards), high / len(shards))
        gain = gain * jnp.repeat(jnp.exp(heights), dims[position] // shards_of).reshape((-1,) + (1,) * (len(dims) - 1 - position))
    return gain


def centred(rng, shape, width, limit, pieces=(), held_as=jnp.bfloat16):
    result = width * jax.random.normal(rng, shape, jnp.float32)
    if pieces:
        result = result * shard_levels(rng, shape, pieces, -0.22, 0.18)
    return jnp.clip(result, -limit, limit).astype(held_as)


def setup_inputs(seed: int = 0) -> dict:
    keys = jax.random.split(jax.random.key(seed), 7)
    operators = centred(keys[0], (NSEL, M, M), 1.0, 6.0, ((0, 4), (1, 8)))
    left_rot = centred(keys[1], (M, M), M ** -0.5, 0.125, ((0, 8),))
    right_rot = centred(keys[2], (M, M), M ** -0.5, 0.125, ((0, 8),))
    integrals = centred(keys[3], (NPQ, NPQ), (NSEL ** -0.5), 1.5, (), jnp.float32)
    pair_index = set_ends(jax.random.randint(keys[4], (NSEL,), 0, NPQ), jax.random.fold_in(keys[4], 1), 0, NPQ - 1).astype(jnp.int32)
    target_index = set_ends(jax.random.randint(keys[5], (NTGT,), 0, NPQ), jax.random.fold_in(keys[5], 1), 0, NPQ - 1).astype(jnp.int32)
    return dict(operators=operators, left_rot=left_rot, right_rot=right_rot, integrals=integrals, pair_index=pair_index, target_index=target_index)


def rotate_one(single, left_rot, right_rot):
    half_rot = jnp.dot(single, right_rot, preferred_element_type=jnp.float32).astype(jnp.bfloat16)
    return jnp.dot(left_rot.T, half_rot, preferred_element_type=jnp.float32).astype(jnp.bfloat16)


def reference(operators, left_rot, right_rot, integrals, pair_index, target_index):
    rotated = lax.map(lambda single: rotate_one(single, left_rot, right_rot), operators)
    coupling = integrals[target_index.astype(jnp.int32)][:, pair_index.astype(jnp.int32)].astype(jnp.bfloat16)
    weights = coupling.astype(jnp.float32)

    def assemble(row_weights):
        return jnp.einsum("k,kmn->mn", row_weights, rotated.astype(jnp.float32)).astype(jnp.bfloat16)

    return lax.map(assemble, weights)
```

```python
import functools

import jax
import jax.numpy as jnp
from jax import lax
from jax.experimental import pallas as pl
from jax.experimental.pallas import tpu as pltpu
from jax.sharding import PartitionSpec as P

CORES = 2
NEAR = 2
BLOCK = 16
MESH_ID = pl.DeviceIdType.MESH


def flip(index, offset, count):
    total, bit = 0, 1
    while bit < count:
        total = total + bit * ((index // bit + offset // bit) % 2)
        bit *= 2
    return total


def kernel(npair, nline, offsets, a_hbm, r_hbm, lt_hbm, kron_ref, out_hbm,
           a_ref, r_ref, lt_ref, h_ref, g_ref, x_ref, y_ref, z_ref, acc_ref, stage_ref,
           load_sem, line_send, line_recv, plane_send, plane_recv, core_send, core_recv,
           swap_send, swap_recv, in_send, in_recv, out_send, out_recv, store_sem):
    own, rows, cols = a_hbm.shape
    ntg = own
    nmat = nline * CORES
    width = cols // nmat
    strip = rows // npair
    mpiece = cols // npair
    pair, mat = lax.axis_index("pair"), lax.axis_index("mat")
    line, core = mat // CORES, mat % CORES
    peers = tuple(range(1, npair))
    straight = tuple(e for e in peers if e % NEAR == 0 or e // NEAR == 0)
    far = tuple(e for e in peers if e not in straight)

    def place(i, f):
        return flip(line, offsets(i), nline) * CORES + flip(core, f, CORES)

    def partner(e):
        return flip(pair, e, npair)

    def remote(src, dst, send, recv, pair_id, mat_id):
        return pltpu.make_async_remote_copy(
            src_ref=src, dst_ref=dst, send_sem=send, recv_sem=recv,
            device_id={"pair": pair_id, "mat": mat_id}, device_id_type=MESH_ID)

    loads = [pltpu.make_async_copy(r_hbm, r_ref.at[pl.ds(0, rows), :], load_sem.at[0]),
             pltpu.make_async_copy(lt_hbm, lt_ref.at[0, :, pl.ds(0, rows)], load_sem.at[1])]
    for s in range(nmat):
        start = pl.multiple_of(place(s // CORES, s % CORES) * rows, rows)
        loads.append(pltpu.make_async_copy(
            a_hbm.at[:, :, pl.ds(start, rows)], a_ref.at[:, :, pl.ds(s * rows, rows)], load_sem.at[2 + s]))
    for copy in loads:
        copy.start()

    barrier = pltpu.get_barrier_semaphore()
    for s in range(1, nmat):
        pl.semaphore_signal(barrier, inc=1, device_id={"pair": pair, "mat": place(s // CORES, s % CORES)},
                            device_id_type=MESH_ID)
    for e in peers:
        pl.semaphore_signal(barrier, inc=1, device_id={"pair": partner(e), "mat": mat}, device_id_type=MESH_ID)
    pl.semaphore_wait(barrier, nmat - 1 + len(peers))

    sibling = place(0, 1)

    def piece(m, i, f, origin, part=None):
        if m == 0:
            at = pl.multiple_of((i * CORES + f) * rows + origin * strip, strip)
            if part is None:
                return r_ref.at[pl.ds(at, strip), :]
            return r_ref.at[pl.ds(at, strip), pl.ds(part * (cols // 2), cols // 2)]
        at = pl.multiple_of(origin * mpiece, mpiece)
        if part is None:
            return lt_ref.at[i, pl.ds(at, mpiece), pl.ds(f * rows, rows)]
        at = pl.multiple_of(at + part * (mpiece // 2), mpiece // 2)
        return lt_ref.at[i, pl.ds(at, mpiece // 2), pl.ds(f * rows, rows)]

    def line_copy(m, i):
        if m == 0:
            src = r_hbm.at[pl.ds(pl.multiple_of(pair * strip, strip), strip), :]
        else:
            src = lt_hbm.at[pl.ds(pl.multiple_of(pair * mpiece, mpiece), mpiece), :]
        return remote(src, piece(m, i, 0, pair), line_send.at[m, i], line_recv.at[m, i], pair, place(i, 0))

    def plane_copy(m, i, to, origin, part=None):
        block = piece(m, i, 0, partner(origin), part)
        k = to ^ origin
        h = 0 if part is None else part
        return remote(block, block, plane_send.at[m, i, k, h], plane_recv.at[m, i, k, h], partner(to), mat)

    def plane_arrival(m, i, e, part=None):
        block = piece(m, i, 0, partner(e), part)
        h = 0 if part is None else part
        return remote(block, block, plane_send.at[m, i, e, h], plane_recv.at[m, i, e, h], partner(e), mat)

    def core_copy(m, i, e):
        return remote(piece(m, i, 0, partner(e)), piece(m, i, 1, partner(e)),
                      core_send.at[m, i, e], core_recv.at[m, i, e], pair, sibling)

    def core_whole(m):
        if m == 0:
            src, dst = r_hbm, r_ref.at[pl.ds(rows, rows), :]
        else:
            src, dst = lt_hbm, lt_ref.at[0, :, pl.ds(rows, rows)]
        return remote(src, dst, core_send.at[m, 0, 0], core_recv.at[m, 0, 0], pair, sibling)

    sent = []

    def launch(copy):
        copy.start()
        sent.append(copy)

    others = tuple(range(1, nline))

    def spread_first(m):
        for i in others:
            line_copy(m, i).wait_recv()
            for e in straight:
                launch(plane_copy(m, i, e, 0))
            launch(core_copy(m, i, 0))

    def spread_second(m):
        for i in others:
            for e in straight:
                plane_arrival(m, i, e).wait_recv()
                for to in straight:
                    if to ^ e in far:
                        launch(plane_copy(m, i, to, e, 0 if e < NEAR else 1))
                launch(core_copy(m, i, e))

    def spread_third(m):
        for i in others:
            for e in far:
                plane_arrival(m, i, e, 0).wait_recv()
                plane_arrival(m, i, e, 1).wait_recv()
                launch(core_copy(m, i, e))

    def spread_last(m):
        core_whole(m).wait_recv()
        for i in others:
            for e in range(npair):
                core_copy(m, i, e).wait_recv()

    for m in range(2):
        for i in others:
            launch(line_copy(m, i))
        launch(core_whole(m))

    spread_first(0)
    spread_second(0)
    spread_first(1)
    spread_third(0)
    for copy in loads:
        copy.wait()
    spread_last(0)

    def swap_copy(s, i, f):
        return remote(h_ref.at[s], g_ref.at[s], swap_send.at[s], swap_recv.at[s], pair, place(i, f))

    def half(i, f):
        start = pl.multiple_of(place(i, f) * width, width)
        block = jnp.dot(a_ref[...].reshape(own * rows, cols), r_ref[:, pl.ds(start, width)],
                        preferred_element_type=jnp.float32)
        return block.astype(jnp.bfloat16).reshape(own, rows, width)

    def rotate(s, carry):
        i, f = s // CORES, s % CORES
        h_ref[s] = half(i, f)
        swap_copy(s, i, f).start()
        return carry

    lax.fori_loop(CORES, 2 * CORES, rotate, 0)
    g_ref[0] = half(0, 0)
    lax.fori_loop(1, CORES, rotate, 0)
    lax.fori_loop(2 * CORES, nmat, rotate, 0)

    def in_copy(s, e):
        rows_of = pl.ds(pl.multiple_of(partner(e) * strip, strip), strip)
        return remote(g_ref.at[s, :, rows_of, :], x_ref.at[s, pair], in_send.at[s, e], in_recv.at[s, e],
                      partner(e), mat)

    def in_local(s):
        rows_of = pl.ds(pl.multiple_of(pair * strip, strip), strip)
        return pltpu.make_async_copy(g_ref.at[s, :, rows_of, :], x_ref.at[s, pair], in_recv.at[s, 0])

    def out_rows(s):
        at = (s % CORES) * rows + pair * strip
        return z_ref.at[s // CORES, :, pl.ds(pl.multiple_of(at, strip), strip), :]

    def out_copy(s, e):
        return remote(y_ref.at[s, partner(e)], out_rows(s), out_send.at[s, e], out_recv.at[s, e], partner(e), mat)

    def out_local(s):
        return pltpu.make_async_copy(y_ref.at[s, pair], out_rows(s), out_recv.at[s, 0])

    def enter(s):
        if s > 0:
            swap_copy(s, s // CORES, s % CORES).wait_recv()
        for e in peers[::-1]:
            launch(in_copy(s, e))
        in_local(s).start()

    def mix(s):
        for e in peers:
            in_copy(s, e).wait_recv()
        in_local(s).wait()

        def chunk(b, carry):
            at = pl.ds(pl.multiple_of(b * BLOCK, BLOCK), BLOCK)
            block = x_ref[s, :, :, at, :].reshape(npair * own * BLOCK, width)
            mixed = jnp.dot(kron_ref[...], block, preferred_element_type=jnp.float32)
            y_ref[s, :, :, at, :] = mixed.astype(jnp.bfloat16).reshape(npair, ntg, BLOCK, width)
            return carry

        lax.fori_loop(0, strip // BLOCK, chunk, 0)
        for e in peers[::-1]:
            launch(out_copy(s, e))
        out_local(s).start()

    tile = min(512, cols)

    def finish(i):
        for f in range(CORES):
            for e in peers:
                out_copy(i * CORES + f, e).wait_recv()
            out_local(i * CORES + f).wait()

        def target(n, carry):
            t, at = n // (cols // tile), pl.ds(pl.multiple_of(n % (cols // tile) * tile, tile), tile)
            part = jnp.dot(lt_ref[i, at, :], z_ref[i, t], preferred_element_type=jnp.float32)
            if i > 0:
                part = part + acc_ref[t, at, :]
            if i < nline - 1:
                acc_ref[t, at, :] = part
            else:
                stage_ref[t, at, :] = part.astype(jnp.bfloat16)
            return carry

        steps = cols // tile
        if i < nline - 1:
            lax.fori_loop(0, ntg * steps, target, 0)
        else:
            for t in range(ntg):
                lax.fori_loop(t * steps, (t + 1) * steps, target, 0)
                pltpu.make_async_copy(stage_ref.at[t], out_hbm.at[t], store_sem.at[t]).start()

    for s in range(nmat + 1):
        if s < nmat:
            enter(s)
        if s == 1:
            spread_second(1)
        if s == 3:
            spread_third(1)
            spread_last(1)
        if s > 0:
            mix(s - 1)
        if s > CORES and s % CORES == 1:
            finish((s - CORES - 1) // CORES)
    finish(nline - 1)

    for s in range(1, nmat):
        swap_copy(s, s // CORES, s % CORES).wait_send()
    for copy in sent:
        copy.wait_send()
    for t in range(ntg):
        pltpu.make_async_copy(stage_ref.at[t], out_hbm.at[t], store_sem.at[t]).wait()


def selector(indices, count):
    return (indices[:, None] == jnp.arange(count, dtype=jnp.int32)[None, :]).astype(jnp.float32)


def shards(operators, left_rot, right_rot, integrals, pair_index, target_index):
    npairs = integrals.shape[0]
    npair, nmat = lax.axis_size("pair"), lax.axis_size("mat")
    nline = nmat // CORES
    own, rows, cols = operators.shape
    width = cols // nmat
    strip = rows // npair
    ntgt, nsel = target_index.shape[0], pair_index.shape[0]
    ntg = ntgt // npair

    rowsel = jnp.dot(selector(target_index, npairs), integrals, precision=lax.Precision.HIGHEST)
    coupling = jnp.dot(
        rowsel, selector(pair_index, npairs).T, precision=lax.Precision.HIGHEST
    ).astype(jnp.bfloat16)
    kron = jnp.kron(coupling, jnp.eye(BLOCK, dtype=jnp.bfloat16))

    def offsets(i):
        if isinstance(i, int):
            return 0 if i == 0 else (nline - 1 - (i - 1) // 2 if i % 2 == 1 else i // 2)
        odd = i % 2
        return odd * (nline - 1 - (i - 1) // 2) + (1 - odd) * (i // 2)

    nslot = nmat
    bf16 = jnp.bfloat16
    dma = pltpu.SemaphoreType.DMA
    anywhere = pl.BlockSpec(memory_space=pl.ANY)
    return pl.pallas_call(
        functools.partial(kernel, npair, nline, offsets),
        out_shape=jax.ShapeDtypeStruct((ntg, cols, width), bf16),
        in_specs=[anywhere, anywhere, anywhere, pl.BlockSpec(memory_space=pltpu.VMEM)],
        out_specs=anywhere,
        scratch_shapes=[
            pltpu.VMEM((own, rows, cols), bf16),
            pltpu.VMEM((cols, cols), bf16),
            pltpu.VMEM((nline, cols, CORES * rows), bf16),
            pltpu.VMEM((nslot, own, rows, width), bf16),
            pltpu.VMEM((nslot, own, rows, width), bf16),
            pltpu.VMEM((nslot, npair, own, strip, width), bf16),
            pltpu.VMEM((nslot, npair, ntg, strip, width), bf16),
            pltpu.VMEM((nline, ntg, CORES * rows, width), bf16),
            pltpu.VMEM((ntg, cols, width), jnp.float32),
            pltpu.VMEM((ntg, cols, width), bf16),
            dma((2 + nslot,)),
            dma((2, nline)), dma((2, nline)),
            dma((2, nline, npair, 2)), dma((2, nline, npair, 2)),
            dma((2, nline, npair)), dma((2, nline, npair)),
            dma((nslot,)), dma((nslot,)),
            dma((nslot, npair)), dma((nslot, npair)),
            dma((nslot, npair)), dma((nslot, npair)),
            dma((ntg,)),
        ],
        compiler_params=pltpu.CompilerParams(
            collective_id=0, has_side_effects=True, vmem_limit_bytes=67043328),
    )(operators, right_rot, left_rot.T, kron)


def solution(mesh):
    in_specs = (P("pair", "mat", None), P("mat", None), P("mat", None), P(), P(), P())
    out_specs = P("pair", None, "mat")
    return jax.shard_map(shards, mesh=mesh, in_specs=in_specs, out_specs=out_specs, check_vma=False)
```

```python
import functools

import jax
import jax.numpy as jnp
from jax import lax
from jax.experimental import pallas as pl
from jax.experimental.pallas import tpu as pltpu
from jax.sharding import PartitionSpec as P

CORES = 2
NEAR = 2
BLOCK = 16
RIGHT, LEFT = 0, 1
UP, DOWN = 0, 1
MESH_ID = pl.DeviceIdType.MESH


def flip(index, offset, count):
    total, bit = 0, 1
    while bit < count:
        total = total + bit * ((index // bit + offset // bit) % 2)
        bit *= 2
    return total


def offset_of(i, nline):
    if isinstance(i, int):
        return 0 if i == 0 else (nline - 1 - (i - 1) // 2 if i % 2 == 1 else i // 2)
    odd = i % 2
    return odd * (nline - 1 - (i - 1) // 2) + (1 - odd) * (i // 2)


def kernel(npair, nline, targets_ref, pairs_ref, a_hbm, r_hbm, l_hbm, integrals_hbm, out_hbm,
           a_ref, r_ref, l_ref, lt_ref, integrals_ref, rows_ref, kron_ref, h_ref, g_ref, x_ref, y_ref, z_ref,
           acc_ref, stage_ref,
           load_sem, line_send, line_recv, plane_send, plane_recv, core_send, core_recv,
           swap_send, swap_recv, in_send, in_recv, out_send, out_recv, store_sem):
    own, rows, cols = a_hbm.shape
    ntgt, nsel = targets_ref.shape[0], pairs_ref.shape[0]
    ntg = ntgt // npair
    nmat = nline * CORES
    width = cols // nmat
    strip = rows // npair
    mpiece = cols // npair
    pair, mat = lax.axis_index("pair"), lax.axis_index("mat")
    line, core = mat // CORES, mat % CORES
    peers = tuple(range(1, npair))
    straight = tuple(e for e in peers if e % NEAR == 0 or e // NEAR == 0)
    far = tuple(e for e in peers if e not in straight)
    hops = range(1, nline)

    def place(i, f):
        return flip(line, offset_of(i, nline), nline) * CORES + flip(core, f, CORES)

    def partner(e):
        return flip(pair, e, npair)

    sibling = line * CORES + flip(core, 1, CORES)

    def remote(src, dst, send, recv, pair_id, mat_id):
        return pltpu.make_async_remote_copy(
            src_ref=src, dst_ref=dst, send_sem=send, recv_sem=recv,
            device_id={"pair": pair_id, "mat": mat_id}, device_id_type=MESH_ID)

    sent = []

    def launch(make, cond=None):
        sent.append((make, cond))
        if cond is None:
            make().start()
        else:
            pl.when(cond)(lambda: make().start())

    load_r = pltpu.make_async_copy(r_hbm, r_ref.at[pl.ds(pl.multiple_of(mat * rows, rows), rows), :], load_sem.at[0])
    load_l = pltpu.make_async_copy(l_hbm, l_ref, load_sem.at[1])
    load_i = pltpu.make_async_copy(integrals_hbm, integrals_ref, load_sem.at[2])
    load_a = pltpu.make_async_copy(a_hbm, a_ref, load_sem.at[3])
    for copy in (load_l, load_i, load_r, load_a):
        copy.start()

    barrier = pltpu.get_barrier_semaphore()
    for s in range(1, nmat):
        pl.semaphore_signal(barrier, inc=1, device_id={"pair": pair, "mat": place(s // CORES, s % CORES)},
                            device_id_type=MESH_ID)
    for e in peers:
        pl.semaphore_signal(barrier, inc=1, device_id={"pair": partner(e), "mat": mat}, device_id_type=MESH_ID)
    pl.semaphore_wait(barrier, nmat - 1 + len(peers))

    def piece(m, source, c, origin, part=None):
        if m == RIGHT:
            at = pl.multiple_of((source * CORES + c) * rows + origin * strip, strip)
            if part is None:
                return r_ref.at[pl.ds(at, strip), :]
            return r_ref.at[pl.ds(at, strip), pl.ds(part * (cols // 2), cols // 2)]
        lanes = pl.ds(pl.multiple_of(c * rows, rows), rows)
        at = pl.multiple_of(origin * mpiece, mpiece)
        if part is None:
            return lt_ref.at[source, pl.ds(at, mpiece), lanes]
        at = pl.multiple_of(at + part * (mpiece // 2), mpiece // 2)
        return lt_ref.at[source, pl.ds(at, mpiece // 2), lanes]

    def own_piece(m):
        if m == RIGHT:
            return r_hbm.at[pl.ds(pl.multiple_of(pair * strip, strip), strip), :]
        return piece(LEFT, line, core, pair)

    def chain_copy(m, source, way, first):
        block = piece(m, source, core, pair)
        step = 1 if way == UP else -1
        return remote(own_piece(m) if first else block, block, line_send.at[m, source, way], line_recv.at[m, source],
                      pair, (line + step) * CORES + core)

    def line_copy(m, i):
        other = place(i, 0)
        return remote(own_piece(m), piece(m, line, core, pair), line_send.at[m, other // CORES, UP],
                      line_recv.at[m, line], pair, other)

    def line_arrival(m, source):
        block = piece(m, source, core, pair)
        return remote(block, block, line_send.at[m, source, UP], line_recv.at[m, source], pair, sibling)

    def plane_copy(m, source, to, origin, part=None):
        block = piece(m, source, core, partner(origin), part)
        k, h = to ^ origin, 0 if part is None else part
        return remote(block, block, plane_send.at[m, source, k, h], plane_recv.at[m, source, k, h], partner(to), mat)

    def plane_arrival(m, source, e, part=None):
        block = piece(m, source, core, partner(e), part)
        h = 0 if part is None else part
        return remote(block, block, plane_send.at[m, source, e, h], plane_recv.at[m, source, e, h], partner(e), mat)

    def core_copy(m, source, e, mine=True):
        block = piece(m, source, core if mine else flip(core, 1, CORES), partner(e))
        return remote(block, block, core_send.at[m, source, e], core_recv.at[m, source, e], pair, sibling)

    def core_whole(m):
        if m == RIGHT:
            src, dst = r_hbm, r_ref.at[pl.ds(pl.multiple_of(mat * rows, rows), rows), :]
        else:
            src = dst = lt_ref.at[line, :, pl.ds(pl.multiple_of(core * rows, rows), rows)]
        return remote(src, dst, core_send.at[m, line, 0], core_recv.at[m, line, 0], pair, sibling)

    def reaches(way, h):
        if way == UP:
            return line >= h, line - h
        return line + h < nline, line + h

    def both(h, act):
        for way in (UP, DOWN):
            cond, source = reaches(way, h)
            act(way, cond, source)

    def spread_first(m, h):
        def act(way, cond, source):
            pl.when(cond)(lambda: line_arrival(m, source).wait_recv())
            if m == RIGHT and h + 1 < nline:
                more = line < nline - 1 if way == UP else line > 0
                launch(lambda: chain_copy(m, source, way, False), cond & more)
            for e in straight:
                launch(lambda e=e: plane_copy(m, source, e, 0), cond)
            launch(lambda: core_copy(m, source, 0), cond)
        both(h, act)

    def spread_second(m, h):
        def act(way, cond, source):
            for e in straight:
                pl.when(cond)(lambda e=e: plane_arrival(m, source, e).wait_recv())
                for to in straight:
                    if to ^ e in far:
                        launch(lambda e=e, to=to: plane_copy(m, source, to, e, 0 if e < NEAR else 1), cond)
                launch(lambda e=e: core_copy(m, source, e), cond)
        both(h, act)

    def spread_third(m, h):
        def act(way, cond, source):
            for e in far:
                for part in range(2):
                    pl.when(cond)(lambda e=e, part=part: plane_arrival(m, source, e, part).wait_recv())
                launch(lambda e=e: core_copy(m, source, e), cond)
        both(h, act)

    def spread_last(m, h):
        def act(way, cond, source):
            for e in range(npair):
                pl.when(cond)(lambda e=e: core_copy(m, source, e, False).wait_recv())
        both(h, act)

    launch(lambda: chain_copy(RIGHT, line, UP, True), line < nline - 1)
    launch(lambda: chain_copy(RIGHT, line, DOWN, True), line > 0)
    launch(lambda: core_whole(RIGHT))

    load_l.wait()
    lanes = pl.ds(pl.multiple_of(core * rows, rows), rows)

    def turn(b, carry):
        at = pl.ds(pl.multiple_of(b * 256, 256), 256)
        lt_ref[line, at, lanes] = l_ref[:, at].T
        return carry

    lax.fori_loop(0, cols // 256, turn, 0)

    load_i.wait()
    for t in range(ntgt):
        rows_ref[pl.ds(t, 1), :] = integrals_ref[pl.ds(targets_ref[t], 1), :]
    picked = rows_ref[...]
    lane = lax.broadcasted_iota(jnp.int32, picked.shape, 1)
    column = lax.broadcasted_iota(jnp.int32, (ntgt, nsel), 1)
    coupling = jnp.zeros((ntgt, nsel), jnp.float32)
    for k in range(nsel):
        value = jnp.sum(jnp.where(lane == pairs_ref[k], picked, 0.0), axis=1, keepdims=True)
        coupling = jnp.where(column == k, value, coupling)
    down = lax.broadcasted_iota(jnp.int32, (ntgt * BLOCK, ntgt), 0) // BLOCK
    tall = (down == lax.broadcasted_iota(jnp.int32, (ntgt * BLOCK, ntgt), 1)).astype(jnp.bfloat16)
    across = lax.broadcasted_iota(jnp.int32, (nsel, nsel * BLOCK), 1) // BLOCK
    broad = (across == lax.broadcasted_iota(jnp.int32, (nsel, nsel * BLOCK), 0)).astype(jnp.bfloat16)
    wide = jnp.dot(coupling.astype(jnp.bfloat16), broad, preferred_element_type=jnp.float32).astype(jnp.bfloat16)
    full = jnp.dot(tall, wide, preferred_element_type=jnp.float32)
    same = (lax.broadcasted_iota(jnp.int32, full.shape, 0) % BLOCK
            == lax.broadcasted_iota(jnp.int32, full.shape, 1) % BLOCK)
    kron_ref[...] = jnp.where(same, full, 0.0).astype(jnp.bfloat16)

    for h in range(1, nline + 2):
        if h < nline:
            spread_first(RIGHT, h)
        if h == nline - 1:
            for i in hops:
                launch(lambda i=i: line_copy(LEFT, i))
            launch(lambda: core_whole(LEFT))
        if 1 <= h - 1 < nline:
            spread_second(RIGHT, h - 1)
        if 1 <= h - 2 < nline:
            spread_third(RIGHT, h - 2)
    load_r.wait()
    load_a.wait()
    core_whole(RIGHT).wait_recv()
    for h in hops:
        spread_last(RIGHT, h)

    def swap_copy(s, i, f):
        return remote(h_ref.at[s], g_ref.at[s], swap_send.at[s], swap_recv.at[s], pair, place(i, f))

    def half(i, f):
        start = pl.multiple_of(place(i, f) * width, width)
        block = jnp.dot(a_ref[...].reshape(own * rows, cols), r_ref[:, pl.ds(start, width)],
                        preferred_element_type=jnp.float32)
        return block.astype(jnp.bfloat16).reshape(own, rows, width)

    def rotate(s, carry):
        i, f = s // CORES, s % CORES
        h_ref[s] = half(i, f)
        swap_copy(s, i, f).start()
        return carry

    def in_copy(s, e):
        rows_of = pl.ds(pl.multiple_of(partner(e) * strip, strip), strip)
        return remote(g_ref.at[s, :, rows_of, :], x_ref.at[s, pair], in_send.at[s, e], in_recv.at[s, e],
                      partner(e), mat)

    def in_local(s):
        rows_of = pl.ds(pl.multiple_of(pair * strip, strip), strip)
        return pltpu.make_async_copy(g_ref.at[s, :, rows_of, :], x_ref.at[s, pair], in_recv.at[s, 0])

    def out_rows(s):
        at = flip(core, s % CORES, CORES) * rows + pair * strip
        return z_ref.at[s // CORES, :, pl.ds(pl.multiple_of(at, strip), strip), :]

    def out_copy(s, e):
        return remote(y_ref.at[s, partner(e)], out_rows(s), out_send.at[s, e], out_recv.at[s, e], partner(e), mat)

    def out_local(s):
        return pltpu.make_async_copy(y_ref.at[s, pair], out_rows(s), out_recv.at[s, 0])

    def enter(s):
        if s > 0:
            swap_copy(s, s // CORES, s % CORES).wait_recv()
        for e in peers[::-1]:
            launch(lambda e=e: in_copy(s, e))
        in_local(s).start()

    def mix(s):
        for e in peers:
            in_copy(s, e).wait_recv()
        in_local(s).wait()

        def chunk(b, carry):
            at = pl.ds(pl.multiple_of(b * BLOCK, BLOCK), BLOCK)
            block = x_ref[s, :, :, at, :].reshape(npair * own * BLOCK, width)
            mixed = jnp.dot(kron_ref[...], block, preferred_element_type=jnp.float32)
            y_ref[s, :, :, at, :] = mixed.astype(jnp.bfloat16).reshape(npair, ntg, BLOCK, width)
            return carry

        lax.fori_loop(0, strip // BLOCK, chunk, 0)
        for e in peers[::-1]:
            launch(lambda e=e: out_copy(s, e))
        out_local(s).start()

    tile = min(512, cols)

    def finish(i):
        for f in range(CORES):
            for e in peers:
                out_copy(i * CORES + f, e).wait_recv()
            out_local(i * CORES + f).wait()
        source = flip(line, offset_of(i, nline), nline)

        def target(n, carry):
            t, at = n // (cols // tile), pl.ds(pl.multiple_of(n % (cols // tile) * tile, tile), tile)
            part = jnp.dot(lt_ref[source, at, :], z_ref[i, t], preferred_element_type=jnp.float32)
            if i > 0:
                part = part + acc_ref[t, at, :]
            if i < nline - 1:
                acc_ref[t, at, :] = part
            else:
                stage_ref[t, at, :] = part.astype(jnp.bfloat16)
            return carry

        steps = cols // tile
        if i < nline - 1:
            lax.fori_loop(0, ntg * steps, target, 0)
        else:
            for t in range(ntg):
                lax.fori_loop(t * steps, (t + 1) * steps, target, 0)
                pltpu.make_async_copy(stage_ref.at[t], out_hbm.at[t], store_sem.at[t]).start()

    lax.fori_loop(CORES, CORES + 1, rotate, 0)
    g_ref[0] = half(0, 0)
    enter(0)
    lax.fori_loop(CORES + 1, 2 * CORES, rotate, 0)
    lax.fori_loop(1, CORES, rotate, 0)
    enter(1)
    for h in hops:
        spread_first(LEFT, h)
    lax.fori_loop(2 * CORES, nmat, rotate, 0)

    for i in range(nline):
        first = i * CORES
        if i > 0:
            for f in range(CORES):
                enter(first + f)
        for f in range(CORES):
            mix(first + f)
            if i == 0:
                for h in hops:
                    (spread_second if f == 0 else spread_third)(LEFT, h)
        if i == 1:
            core_whole(LEFT).wait_recv()
            for h in hops:
                spread_last(LEFT, h)
        if i > 0:
            finish(i - 1)
    finish(nline - 1)

    for s in range(1, nmat):
        swap_copy(s, s // CORES, s % CORES).wait_send()
    for make, cond in sent:
        if cond is None:
            make().wait_send()
        else:
            pl.when(cond)(lambda make=make: make().wait_send())
    for t in range(ntg):
        pltpu.make_async_copy(stage_ref.at[t], out_hbm.at[t], store_sem.at[t]).wait()


def shards(operators, left_rot, right_rot, integrals, pair_index, target_index):
    npair, nmat = lax.axis_size("pair"), lax.axis_size("mat")
    nline = nmat // CORES
    own, rows, cols = operators.shape
    width = cols // nmat
    strip = rows // npair
    ntgt, nsel = target_index.shape[0], pair_index.shape[0]
    ntg = ntgt // npair
    bf16, f32 = jnp.bfloat16, jnp.float32
    dma = pltpu.SemaphoreType.DMA
    anywhere = pl.BlockSpec(memory_space=pl.ANY)
    scalars = pl.BlockSpec(memory_space=pltpu.SMEM)
    return pl.pallas_call(
        functools.partial(kernel, npair, nline),
        out_shape=jax.ShapeDtypeStruct((ntg, cols, width), bf16),
        in_specs=[scalars, scalars, anywhere, anywhere, anywhere, anywhere],
        out_specs=anywhere,
        scratch_shapes=[
            pltpu.VMEM((own, rows, cols), bf16),
            pltpu.VMEM((cols, cols), bf16),
            pltpu.VMEM((rows, cols), bf16),
            pltpu.VMEM((nline, cols, CORES * rows), bf16),
            pltpu.VMEM(integrals.shape, f32),
            pltpu.VMEM((ntgt, integrals.shape[1]), f32),
            pltpu.VMEM((ntgt * BLOCK, nsel * BLOCK), bf16),
            pltpu.VMEM((nmat, own, rows, width), bf16),
            pltpu.VMEM((nmat, own, rows, width), bf16),
            pltpu.VMEM((nmat, npair, own, strip, width), bf16),
            pltpu.VMEM((nmat, npair, ntg, strip, width), bf16),
            pltpu.VMEM((nline, ntg, CORES * rows, width), bf16),
            pltpu.VMEM((ntg, cols, width), f32),
            pltpu.VMEM((ntg, cols, width), bf16),
            dma((4,)),
            dma((2, nline, 2)), dma((2, nline)),
            dma((2, nline, npair, 2)), dma((2, nline, npair, 2)),
            dma((2, nline, npair)), dma((2, nline, npair)),
            dma((nmat,)), dma((nmat,)),
            dma((nmat, npair)), dma((nmat, npair)),
            dma((nmat, npair)), dma((nmat, npair)),
            dma((ntg,)),
        ],
        compiler_params=pltpu.CompilerParams(
            collective_id=0, has_side_effects=True, vmem_limit_bytes=67043328),
    )(target_index, pair_index, operators, right_rot, left_rot, integrals)


def solution(mesh):
    in_specs = (P("pair", "mat", None), P("mat", None), P("mat", None), P(), P(), P())
    out_specs = P("pair", None, "mat")
    return jax.shard_map(shards, mesh=mesh, in_specs=in_specs, out_specs=out_specs, check_vma=False)
```

```python
import functools

import jax
import jax.numpy as jnp
from jax import lax
from jax.experimental import pallas as pl
from jax.experimental.pallas import tpu as pltpu
from jax.sharding import PartitionSpec as P

CORES = 2
NEAR = 2
BLOCK = 16
RIGHT, LEFT = 0, 1
UP, DOWN = 0, 1
MESH_ID = pl.DeviceIdType.MESH


def flip(index, offset, count):
    total, bit = 0, 1
    while bit < count:
        total = total + bit * ((index // bit + offset // bit) % 2)
        bit *= 2
    return total


def offset_of(i, nline):
    if isinstance(i, int):
        return 0 if i == 0 else (nline - 1 - (i - 1) // 2 if i % 2 == 1 else i // 2)
    odd = i % 2
    return odd * (nline - 1 - (i - 1) // 2) + (1 - odd) * (i // 2)


def early_rows(own, ntg, strip):
    return BLOCK if own == ntg and strip > BLOCK else 0


def kernel(npair, nline, targets_ref, pairs_ref, a_hbm, r_hbm, l_hbm, integrals_hbm, out_hbm,
           a_ref, early_ref, r_ref, l_ref, lt_ref, integrals_ref, rows_ref, kron_ref, h_ref, g_ref, x_ref, y_ref, z_ref,
           acc_ref, stage_ref,
           load_sem, line_send, line_recv, plane_send, plane_recv, core_send, core_recv,
           swap_send, swap_recv, first_send, first_recv, in_send, in_recv, pass_send, pass_recv, out_send, out_recv,
           store_sem):
    own, _, strip, cols = a_hbm.shape
    rows = npair * strip
    ntgt, nsel = targets_ref.shape[0], pairs_ref.shape[0]
    ntg = ntgt // npair
    nmat = nline * CORES
    width = cols // nmat
    early = early_rows(own, ntg, strip)
    late = strip - early
    mpiece = cols // npair
    pair, mat = lax.axis_index("pair"), lax.axis_index("mat")
    line, core = mat // CORES, mat % CORES
    peers = tuple(range(1, npair))
    straight = tuple(e for e in peers if e % NEAR == 0 or e // NEAR == 0)
    far = tuple(e for e in peers if e not in straight)
    hops = range(1, nline)

    def place(i, f):
        return flip(line, offset_of(i, nline), nline) * CORES + flip(core, f, CORES)

    def partner(e):
        return flip(pair, e, npair)

    sibling = line * CORES + flip(core, 1, CORES)

    def remote(src, dst, send, recv, pair_id, mat_id):
        return pltpu.make_async_remote_copy(
            src_ref=src, dst_ref=dst, send_sem=send, recv_sem=recv,
            device_id={"pair": pair_id, "mat": mat_id}, device_id_type=MESH_ID)

    sent = []

    def launch(make, cond=None):
        sent.append((make, cond))
        if cond is None:
            make().start()
        else:
            pl.when(cond)(lambda: make().start())

    load_r = pltpu.make_async_copy(r_hbm, r_ref.at[pl.ds(pl.multiple_of(mat * rows, rows), rows), :], load_sem.at[0])
    load_l = pltpu.make_async_copy(l_hbm, l_ref, load_sem.at[1])
    load_i = pltpu.make_async_copy(integrals_hbm, integrals_ref, load_sem.at[2])
    load_a = pltpu.make_async_copy(a_hbm, a_ref, load_sem.at[3])
    for copy in (load_l, load_i, load_r, load_a):
        copy.start()

    barrier = pltpu.get_barrier_semaphore()
    for s in range(1, nmat):
        pl.semaphore_signal(barrier, inc=1, device_id={"pair": pair, "mat": place(s // CORES, s % CORES)},
                            device_id_type=MESH_ID)
    for e in peers:
        pl.semaphore_signal(barrier, inc=1, device_id={"pair": partner(e), "mat": mat}, device_id_type=MESH_ID)
    pl.semaphore_wait(barrier, nmat - 1 + len(peers))

    def piece(m, source, c, origin, part=None):
        if m == RIGHT:
            at = pl.multiple_of((source * CORES + c) * rows + origin * strip, strip)
            if part is None:
                return r_ref.at[pl.ds(at, strip), :]
            return r_ref.at[pl.ds(at, strip), pl.ds(part * (cols // 2), cols // 2)]
        lanes = pl.ds(pl.multiple_of(c * rows, rows), rows)
        at = pl.multiple_of(origin * mpiece, mpiece)
        if part is None:
            return lt_ref.at[source, pl.ds(at, mpiece), lanes]
        at = pl.multiple_of(at + part * (mpiece // 2), mpiece // 2)
        return lt_ref.at[source, pl.ds(at, mpiece // 2), lanes]

    def own_piece(m):
        if m == RIGHT:
            return r_hbm.at[pl.ds(pl.multiple_of(pair * strip, strip), strip), :]
        return piece(LEFT, line, core, pair)

    def chain_copy(m, source, way, first):
        block = piece(m, source, core, pair)
        step = 1 if way == UP else -1
        return remote(own_piece(m) if first else block, block, line_send.at[m, source, way], line_recv.at[m, source],
                      pair, (line + step) * CORES + core)

    def line_arrival(m, source):
        block = piece(m, source, core, pair)
        return remote(block, block, line_send.at[m, source, UP], line_recv.at[m, source], pair, sibling)

    def plane_copy(m, source, to, origin, part=None):
        block = piece(m, source, core, partner(origin), part)
        k, h = to ^ origin, 0 if part is None else part
        return remote(block, block, plane_send.at[m, source, k, h], plane_recv.at[m, source, k, h], partner(to), mat)

    def plane_arrival(m, source, e, part=None):
        block = piece(m, source, core, partner(e), part)
        h = 0 if part is None else part
        return remote(block, block, plane_send.at[m, source, e, h], plane_recv.at[m, source, e, h], partner(e), mat)

    def core_copy(m, source, e, mine=True):
        block = piece(m, source, core if mine else flip(core, 1, CORES), partner(e))
        return remote(block, block, core_send.at[m, source, e], core_recv.at[m, source, e], pair, sibling)

    def core_whole(m):
        if m == RIGHT:
            src, dst = r_hbm, r_ref.at[pl.ds(pl.multiple_of(mat * rows, rows), rows), :]
        else:
            src = dst = lt_ref.at[line, :, pl.ds(pl.multiple_of(core * rows, rows), rows)]
        return remote(src, dst, core_send.at[m, line, 0], core_recv.at[m, line, 0], pair, sibling)

    def reaches(way, h):
        if way == UP:
            return line >= h, line - h
        return line + h < nline, line + h

    def both(h, act):
        for way in (UP, DOWN):
            cond, source = reaches(way, h)
            act(way, cond, source)

    def hop(m, h):
        def act(way, cond, source):
            pl.when(cond)(lambda: line_arrival(m, source).wait_recv())
            if h + 1 < nline:
                more = line < nline - 1 if way == UP else line > 0
                launch(lambda: chain_copy(m, source, way, False), cond & more)
        both(h, act)

    def spread_first(m, h):
        def act(way, cond, source):
            for e in straight:
                launch(lambda e=e: plane_copy(m, source, e, 0), cond)
            launch(lambda: core_copy(m, source, 0), cond)
        both(h, act)

    def spread_second(m, h):
        def act(way, cond, source):
            for e in straight:
                pl.when(cond)(lambda e=e: plane_arrival(m, source, e).wait_recv())
                for to in straight:
                    if to ^ e in far:
                        launch(lambda e=e, to=to: plane_copy(m, source, to, e, 0 if e < NEAR else 1), cond)
                launch(lambda e=e: core_copy(m, source, e), cond)
        both(h, act)

    def spread_third(m, h):
        def act(way, cond, source):
            for e in far:
                for part in range(2):
                    pl.when(cond)(lambda e=e, part=part: plane_arrival(m, source, e, part).wait_recv())
                launch(lambda e=e: core_copy(m, source, e), cond)
        both(h, act)

    def spread_last(m, h):
        def act(way, cond, source):
            for e in range(npair):
                pl.when(cond)(lambda e=e: core_copy(m, source, e, False).wait_recv())
        both(h, act)

    def depart(m):
        launch(lambda: chain_copy(m, line, UP, True), line < nline - 1)
        launch(lambda: chain_copy(m, line, DOWN, True), line > 0)
        launch(lambda: core_whole(m))

    def early_source(position):
        return a_hbm.at[:, position, pl.ds(0, early), :]

    def early_copy(e):
        return remote(early_source(partner(e)), early_ref.at[pair], first_send.at[e], first_recv.at[e],
                      partner(e), mat)

    def early_mix():
        for e in peers:
            early_copy(e).wait_recv()
        early_local.wait()
        load_a.wait()
        span = min(512, cols)

        def columns(b, carry):
            at = pl.ds(pl.multiple_of(b * span, span), span)
            mixed = jnp.dot(kron_ref[...], early_ref[:, :, :, at].reshape(nsel * BLOCK, span),
                            preferred_element_type=jnp.float32)
            mixed = mixed.astype(jnp.bfloat16).reshape(npair, ntg, BLOCK, span)
            for position in range(npair):
                a_ref[:, position, pl.ds(0, early), at] = mixed[position]
            return carry

        lax.fori_loop(0, cols // span, columns, 0)

    depart(RIGHT)
    if early:
        for e in peers[::-1]:
            launch(lambda e=e: early_copy(e))
        early_local = pltpu.make_async_copy(early_source(pair), early_ref.at[pair], first_recv.at[0])
        early_local.start()

    load_l.wait()
    lanes = pl.ds(pl.multiple_of(core * rows, rows), rows)

    def turn(b, carry):
        at = pl.ds(pl.multiple_of(b * 256, 256), 256)
        lt_ref[line, at, lanes] = l_ref[:, at].T
        return carry

    lax.fori_loop(0, cols // 256, turn, 0)

    load_i.wait()
    for t in range(ntgt):
        rows_ref[pl.ds(t, 1), :] = integrals_ref[pl.ds(targets_ref[t], 1), :]
    picked = rows_ref[...]
    lane = lax.broadcasted_iota(jnp.int32, picked.shape, 1)
    column = lax.broadcasted_iota(jnp.int32, (ntgt, nsel), 1)
    coupling = jnp.zeros((ntgt, nsel), jnp.float32)
    for k in range(nsel):
        value = jnp.sum(jnp.where(lane == pairs_ref[k], picked, 0.0), axis=1, keepdims=True)
        coupling = jnp.where(column == k, value, coupling)
    down = lax.broadcasted_iota(jnp.int32, (ntgt * BLOCK, ntgt), 0) // BLOCK
    tall = (down == lax.broadcasted_iota(jnp.int32, (ntgt * BLOCK, ntgt), 1)).astype(jnp.bfloat16)
    across = lax.broadcasted_iota(jnp.int32, (nsel, nsel * BLOCK), 1) // BLOCK
    broad = (across == lax.broadcasted_iota(jnp.int32, (nsel, nsel * BLOCK), 0)).astype(jnp.bfloat16)
    wide = jnp.dot(coupling.astype(jnp.bfloat16), broad, preferred_element_type=jnp.float32).astype(jnp.bfloat16)
    full = jnp.dot(tall, wide, preferred_element_type=jnp.float32)
    same = (lax.broadcasted_iota(jnp.int32, full.shape, 0) % BLOCK
            == lax.broadcasted_iota(jnp.int32, full.shape, 1) % BLOCK)
    kron_ref[...] = jnp.where(same, full, 0.0).astype(jnp.bfloat16)

    def right(stage, h):
        if 1 <= h < nline:
            if stage is spread_first:
                hop(RIGHT, h)
            stage(RIGHT, h)

    for h in range(1, nline + 2):
        right(spread_first, h)
        if h == 2:
            depart(LEFT)
        if h == 2 and early:
            early_mix()
        right(spread_second, h - 1)
        if 1 <= h - 2 < nline - 1:
            hop(LEFT, h - 2)
        right(spread_third, h - 2)
    load_r.wait()
    if not early:
        load_a.wait()
    core_whole(RIGHT).wait_recv()
    for h in hops:
        spread_last(RIGHT, h)

    def swap_copy(s, i, f):
        return remote(h_ref.at[s], g_ref.at[s], swap_send.at[s], swap_recv.at[s], pair, place(i, f))

    def half(i, f):
        start = pl.multiple_of(place(i, f) * width, width)
        block = jnp.dot(a_ref[...].reshape(own * rows, cols), r_ref[:, pl.ds(start, width)],
                        preferred_element_type=jnp.float32)
        return block.astype(jnp.bfloat16).reshape(own, npair, strip, width)

    def rotate(s, carry):
        i, f = s // CORES, s % CORES
        h_ref[s] = half(i, f)
        swap_copy(s, i, f).start()
        return carry

    def in_rows(s, position):
        return g_ref.at[s, :, position, pl.ds(early, late), :]

    def in_copy(s, e):
        return remote(in_rows(s, partner(e)), x_ref.at[s, pair], in_send.at[s, e], in_recv.at[s, e], partner(e), mat)

    def in_local(s):
        return pltpu.make_async_copy(in_rows(s, pair), x_ref.at[s, pair], in_recv.at[s, 0])

    def out_rows(s, start, count):
        at = flip(core, s % CORES, CORES) * rows + pair * strip + start
        return z_ref.at[s // CORES, :, pl.ds(pl.multiple_of(at, BLOCK), count), :]

    def pass_copy(s, e):
        return remote(g_ref.at[s, :, partner(e), pl.ds(0, early), :], out_rows(s, 0, early),
                      pass_send.at[s, e], pass_recv.at[s, e], partner(e), mat)

    def pass_local(s):
        return pltpu.make_async_copy(g_ref.at[s, :, pair, pl.ds(0, early), :], out_rows(s, 0, early),
                                     pass_recv.at[s, 0])

    def out_copy(s, e):
        return remote(y_ref.at[s, partner(e)], out_rows(s, early, late), out_send.at[s, e], out_recv.at[s, e],
                      partner(e), mat)

    def out_local(s):
        return pltpu.make_async_copy(y_ref.at[s, pair], out_rows(s, early, late), out_recv.at[s, 0])

    def enter(s):
        if s > 0:
            swap_copy(s, s // CORES, s % CORES).wait_recv()
        for e in peers[::-1]:
            launch(lambda e=e: in_copy(s, e))
        in_local(s).start()
        if early:
            for e in peers[::-1]:
                launch(lambda e=e: pass_copy(s, e))
            pass_local(s).start()

    def mix(s):
        for e in peers:
            in_copy(s, e).wait_recv()
        in_local(s).wait()

        def chunk(b, carry):
            at = pl.ds(pl.multiple_of(b * BLOCK, BLOCK), BLOCK)
            block = x_ref[s, :, :, at, :].reshape(nsel * BLOCK, width)
            mixed = jnp.dot(kron_ref[...], block, preferred_element_type=jnp.float32)
            y_ref[s, :, :, at, :] = mixed.astype(jnp.bfloat16).reshape(npair, ntg, BLOCK, width)
            return carry

        lax.fori_loop(0, late // BLOCK, chunk, 0)
        for e in peers[::-1]:
            launch(lambda e=e: out_copy(s, e))
        out_local(s).start()

    tile = min(512, cols)

    def finish(i):
        for f in range(CORES):
            for e in peers:
                out_copy(i * CORES + f, e).wait_recv()
            out_local(i * CORES + f).wait()
            if early:
                for e in peers:
                    pass_copy(i * CORES + f, e).wait_recv()
                pass_local(i * CORES + f).wait()
        source = flip(line, offset_of(i, nline), nline)

        def target(n, carry):
            t, at = n // (cols // tile), pl.ds(pl.multiple_of(n % (cols // tile) * tile, tile), tile)
            part = jnp.dot(lt_ref[source, at, :], z_ref[i, t], preferred_element_type=jnp.float32)
            if i > 0:
                part = part + acc_ref[t, at, :]
            if i < nline - 1:
                acc_ref[t, at, :] = part
            else:
                stage_ref[t, at, :] = part.astype(jnp.bfloat16)
            return carry

        steps = cols // tile
        if i < nline - 1:
            lax.fori_loop(0, ntg * steps, target, 0)
        else:
            for t in range(ntg):
                lax.fori_loop(t * steps, (t + 1) * steps, target, 0)
                pltpu.make_async_copy(stage_ref.at[t], out_hbm.at[t], store_sem.at[t]).start()

    lax.fori_loop(CORES, 2 * CORES, rotate, 0)
    g_ref[0] = half(0, 0)
    enter(0)
    lax.fori_loop(1, CORES, rotate, 0)
    hop(LEFT, nline - 1)
    for h in hops:
        spread_first(LEFT, h)
    enter(1)
    lax.fori_loop(2 * CORES, nmat, rotate, 0)

    for i in range(nline):
        first = i * CORES
        if i > 0:
            for f in range(CORES):
                enter(first + f)
        for f in range(CORES):
            mix(first + f)
            if i == 0:
                for h in hops:
                    (spread_second if f == 0 else spread_third)(LEFT, h)
        if i == 1:
            core_whole(LEFT).wait_recv()
            for h in hops:
                spread_last(LEFT, h)
        if i > 0:
            finish(i - 1)
    finish(nline - 1)

    for s in range(1, nmat):
        swap_copy(s, s // CORES, s % CORES).wait_send()
    for make, cond in sent:
        if cond is None:
            make().wait_send()
        else:
            pl.when(cond)(lambda make=make: make().wait_send())
    for t in range(ntg):
        pltpu.make_async_copy(stage_ref.at[t], out_hbm.at[t], store_sem.at[t]).wait()


def shards(operators, left_rot, right_rot, integrals, pair_index, target_index):
    npair, nmat = lax.axis_size("pair"), lax.axis_size("mat")
    nline = nmat // CORES
    own, rows, cols = operators.shape
    width = cols // nmat
    strip = rows // npair
    early = early_rows(own, target_index.shape[0] // npair, strip)
    ntgt, nsel = target_index.shape[0], pair_index.shape[0]
    ntg = ntgt // npair
    bf16, f32 = jnp.bfloat16, jnp.float32
    dma = pltpu.SemaphoreType.DMA
    anywhere = pl.BlockSpec(memory_space=pl.ANY)
    scalars = pl.BlockSpec(memory_space=pltpu.SMEM)
    return pl.pallas_call(
        functools.partial(kernel, npair, nline),
        out_shape=jax.ShapeDtypeStruct((ntg, cols, width), bf16),
        in_specs=[scalars, scalars, anywhere, anywhere, anywhere, anywhere],
        out_specs=anywhere,
        scratch_shapes=[
            pltpu.VMEM((own, npair, strip, cols), bf16),
            pltpu.VMEM((npair, own, BLOCK, cols), bf16),
            pltpu.VMEM((cols, cols), bf16),
            pltpu.VMEM((rows, cols), bf16),
            pltpu.VMEM((nline, cols, CORES * rows), bf16),
            pltpu.VMEM(integrals.shape, f32),
            pltpu.VMEM((ntgt, integrals.shape[1]), f32),
            pltpu.VMEM((ntgt * BLOCK, nsel * BLOCK), bf16),
            pltpu.VMEM((nmat, own, npair, strip, width), bf16),
            pltpu.VMEM((nmat, own, npair, strip, width), bf16),
            pltpu.VMEM((nmat, npair, own, strip - early, width), bf16),
            pltpu.VMEM((nmat, npair, ntg, strip - early, width), bf16),
            pltpu.VMEM((nline, ntg, CORES * rows, width), bf16),
            pltpu.VMEM((ntg, cols, width), f32),
            pltpu.VMEM((ntg, cols, width), bf16),
            dma((4,)),
            dma((2, nline, 2)), dma((2, nline)),
            dma((2, nline, npair, 2)), dma((2, nline, npair, 2)),
            dma((2, nline, npair)), dma((2, nline, npair)),
            dma((nmat,)), dma((nmat,)),
            dma((npair,)), dma((npair,)),
            dma((nmat, npair)), dma((nmat, npair)),
            dma((nmat, npair)), dma((nmat, npair)),
            dma((nmat, npair)), dma((nmat, npair)),
            dma((ntg,)),
        ],
        compiler_params=pltpu.CompilerParams(
            collective_id=0, has_side_effects=True, vmem_limit_bytes=67043328),
    )(target_index, pair_index, operators.reshape(own, npair, strip, cols), right_rot, left_rot, integrals)


def solution(mesh):
    in_specs = (P("pair", "mat", None), P("mat", None), P("mat", None), P(), P(), P())
    out_specs = P("pair", None, "mat")
    return jax.shard_map(shards, mesh=mesh, in_specs=in_specs, out_specs=out_specs, check_vma=False)
```

```python
import functools

import jax
import jax.numpy as jnp
from jax import lax
from jax.experimental import pallas as pl
from jax.experimental.pallas import tpu as pltpu
from jax.sharding import PartitionSpec as P

CORES = 2
NEAR = 2
BLOCK = 16
RIGHT, LEFT = 0, 1
UP, DOWN = 0, 1
MESH_ID = pl.DeviceIdType.MESH


def flip(index, offset, count):
    total, bit = 0, 1
    while bit < count:
        total = total + bit * ((index // bit + offset // bit) % 2)
        bit *= 2
    return total


def offset_of(i, nline):
    if isinstance(i, int):
        return 0 if i == 0 else (nline - 1 - (i - 1) // 2 if i % 2 == 1 else i // 2)
    odd = i % 2
    return odd * (nline - 1 - (i - 1) // 2) + (1 - odd) * (i // 2)


def early_rows(own, ntg, strip):
    return BLOCK if own == ntg and strip > BLOCK else 0


def kernel(npair, nline, targets_ref, pairs_ref, a_hbm, r_hbm, l_hbm, integrals_hbm, out_hbm,
           a_ref, early_ref, r_ref, l_ref, lt_ref, integrals_ref, rows_ref, kron_ref, h_ref, g_ref, x_ref, y_ref, z_ref,
           acc_ref, stage_ref,
           load_sem, line_send, line_recv, plane_send, plane_recv, core_send, core_recv,
           swap_send, swap_recv, first_send, first_recv, in_send, in_recv, pass_send, pass_recv, out_send, out_recv,
           store_sem):
    own, _, strip, cols = a_hbm.shape
    rows = npair * strip
    ntgt, nsel = targets_ref.shape[0], pairs_ref.shape[0]
    ntg = ntgt // npair
    nmat = nline * CORES
    width = cols // nmat
    early = early_rows(own, ntg, strip)
    late = strip - early
    mpiece = cols // npair
    pair, mat = lax.axis_index("pair"), lax.axis_index("mat")
    line, core = mat // CORES, mat % CORES
    peers = tuple(range(1, npair))
    straight = tuple(e for e in peers if e % NEAR == 0 or e // NEAR == 0)
    far = tuple(e for e in peers if e not in straight)
    hops = range(1, nline)

    def place(i, f):
        return flip(line, offset_of(i, nline), nline) * CORES + flip(core, f, CORES)

    def partner(e):
        return flip(pair, e, npair)

    sibling = line * CORES + flip(core, 1, CORES)

    def remote(src, dst, send, recv, pair_id, mat_id):
        return pltpu.make_async_remote_copy(
            src_ref=src, dst_ref=dst, send_sem=send, recv_sem=recv,
            device_id={"pair": pair_id, "mat": mat_id}, device_id_type=MESH_ID)

    sent = []

    def launch(make, cond=None):
        sent.append((make, cond))
        if cond is None:
            make().start()
        else:
            pl.when(cond)(lambda: make().start())

    load_r = pltpu.make_async_copy(r_hbm, r_ref.at[pl.ds(pl.multiple_of(mat * rows, rows), rows), :], load_sem.at[0])
    load_l = pltpu.make_async_copy(l_hbm, l_ref, load_sem.at[1])
    load_i = pltpu.make_async_copy(integrals_hbm, integrals_ref, load_sem.at[2])
    load_a = pltpu.make_async_copy(a_hbm, a_ref, load_sem.at[3])
    for copy in (load_l, load_i, load_r, load_a):
        copy.start()

    barrier = pltpu.get_barrier_semaphore()
    for s in range(1, nmat):
        pl.semaphore_signal(barrier, inc=1, device_id={"pair": pair, "mat": place(s // CORES, s % CORES)},
                            device_id_type=MESH_ID)
    for e in peers:
        pl.semaphore_signal(barrier, inc=1, device_id={"pair": partner(e), "mat": mat}, device_id_type=MESH_ID)
    pl.semaphore_wait(barrier, nmat - 1 + len(peers))

    def piece(m, source, c, origin, part=None):
        if m == RIGHT:
            at = pl.multiple_of((source * CORES + c) * rows + origin * strip, strip)
            if part is None:
                return r_ref.at[pl.ds(at, strip), :]
            return r_ref.at[pl.ds(at, strip), pl.ds(part * (cols // 2), cols // 2)]
        lanes = pl.ds(pl.multiple_of(c * rows, rows), rows)
        at = pl.multiple_of(origin * mpiece, mpiece)
        if part is None:
            return lt_ref.at[source, pl.ds(at, mpiece), lanes]
        at = pl.multiple_of(at + part * (mpiece // 2), mpiece // 2)
        return lt_ref.at[source, pl.ds(at, mpiece // 2), lanes]

    def own_piece(m):
        if m == RIGHT:
            return r_hbm.at[pl.ds(pl.multiple_of(pair * strip, strip), strip), :]
        return piece(LEFT, line, core, pair)

    def chain_copy(m, source, way, first):
        block = piece(m, source, core, pair)
        step = 1 if way == UP else -1
        return remote(own_piece(m) if first else block, block, line_send.at[m, source, way], line_recv.at[m, source],
                      pair, (line + step) * CORES + core)

    def line_arrival(m, source):
        block = piece(m, source, core, pair)
        return remote(block, block, line_send.at[m, source, UP], line_recv.at[m, source], pair, sibling)

    def plane_copy(m, source, to, origin, part=None):
        block = piece(m, source, core, partner(origin), part)
        k, h = to ^ origin, 0 if part is None else part
        return remote(block, block, plane_send.at[m, source, k, h], plane_recv.at[m, source, k, h], partner(to), mat)

    def plane_arrival(m, source, e, part=None):
        block = piece(m, source, core, partner(e), part)
        h = 0 if part is None else part
        return remote(block, block, plane_send.at[m, source, e, h], plane_recv.at[m, source, e, h], partner(e), mat)

    def core_copy(m, source, e, mine=True):
        block = piece(m, source, core if mine else flip(core, 1, CORES), partner(e))
        return remote(block, block, core_send.at[m, source, e], core_recv.at[m, source, e], pair, sibling)

    def core_whole(m):
        if m == RIGHT:
            src, dst = r_hbm, r_ref.at[pl.ds(pl.multiple_of(mat * rows, rows), rows), :]
        else:
            src = dst = lt_ref.at[line, :, pl.ds(pl.multiple_of(core * rows, rows), rows)]
        return remote(src, dst, core_send.at[m, line, 0], core_recv.at[m, line, 0], pair, sibling)

    def reaches(way, h):
        if way == UP:
            return line >= h, line - h
        return line + h < nline, line + h

    def both(h, act):
        for way in (UP, DOWN):
            cond, source = reaches(way, h)
            act(way, cond, source)

    def hop(m, h):
        def act(way, cond, source):
            pl.when(cond)(lambda: line_arrival(m, source).wait_recv())
            if h + 1 < nline:
                more = line < nline - 1 if way == UP else line > 0
                launch(lambda: chain_copy(m, source, way, False), cond & more)
        both(h, act)

    def spread_first(m, h):
        def act(way, cond, source):
            for e in straight:
                launch(lambda e=e: plane_copy(m, source, e, 0), cond)
            launch(lambda: core_copy(m, source, 0), cond)
        both(h, act)

    def spread_second(m, h):
        def act(way, cond, source):
            for e in straight:
                pl.when(cond)(lambda e=e: plane_arrival(m, source, e).wait_recv())
                for to in straight:
                    if to ^ e in far:
                        launch(lambda e=e, to=to: plane_copy(m, source, to, e, 0 if e < NEAR else 1), cond)
                launch(lambda e=e: core_copy(m, source, e), cond)
        both(h, act)

    def spread_third(m, h):
        def act(way, cond, source):
            for e in far:
                for part in range(2):
                    pl.when(cond)(lambda e=e, part=part: plane_arrival(m, source, e, part).wait_recv())
                launch(lambda e=e: core_copy(m, source, e), cond)
        both(h, act)

    def spread_last(m, h):
        def act(way, cond, source):
            for e in range(npair):
                pl.when(cond)(lambda e=e: core_copy(m, source, e, False).wait_recv())
        both(h, act)

    def depart(m):
        launch(lambda: chain_copy(m, line, UP, True), line < nline - 1)
        launch(lambda: chain_copy(m, line, DOWN, True), line > 0)
        launch(lambda: core_whole(m))

    def early_source(position):
        return a_hbm.at[:, position, pl.ds(0, early), :]

    def early_copy(e):
        return remote(early_source(partner(e)), early_ref.at[pair], first_send.at[e], first_recv.at[e],
                      partner(e), mat)

    def early_mix():
        for e in peers:
            early_copy(e).wait_recv()
        early_local.wait()
        load_a.wait()
        span = min(512, cols)

        def columns(b, carry):
            at = pl.ds(pl.multiple_of(b * span, span), span)
            mixed = jnp.dot(kron_ref[...], early_ref[:, :, :, at].reshape(nsel * BLOCK, span),
                            preferred_element_type=jnp.float32)
            mixed = mixed.astype(jnp.bfloat16).reshape(npair, ntg, BLOCK, span)
            for position in range(npair):
                a_ref[:, position, pl.ds(0, early), at] = mixed[position]
            return carry

        lax.fori_loop(0, cols // span, columns, 0)

    depart(RIGHT)
    if early:
        for e in peers[::-1]:
            launch(lambda e=e: early_copy(e))
        early_local = pltpu.make_async_copy(early_source(pair), early_ref.at[pair], first_recv.at[0])
        early_local.start()

    load_l.wait()
    lanes = pl.ds(pl.multiple_of(core * rows, rows), rows)

    def turn(b, carry):
        at = pl.ds(pl.multiple_of(b * 256, 256), 256)
        lt_ref[line, at, lanes] = l_ref[:, at].T
        return carry

    lax.fori_loop(0, cols // 256, turn, 0)

    load_i.wait()
    for t in range(ntgt):
        rows_ref[pl.ds(t, 1), :] = integrals_ref[pl.ds(targets_ref[t], 1), :]
    picked = rows_ref[...]
    lane = lax.broadcasted_iota(jnp.int32, picked.shape, 1)
    column = lax.broadcasted_iota(jnp.int32, (ntgt, nsel), 1)
    coupling = jnp.zeros((ntgt, nsel), jnp.float32)
    for k in range(nsel):
        value = jnp.sum(jnp.where(lane == pairs_ref[k], picked, 0.0), axis=1, keepdims=True)
        coupling = jnp.where(column == k, value, coupling)
    down = lax.broadcasted_iota(jnp.int32, (ntgt * BLOCK, ntgt), 0) // BLOCK
    tall = (down == lax.broadcasted_iota(jnp.int32, (ntgt * BLOCK, ntgt), 1)).astype(jnp.bfloat16)
    across = lax.broadcasted_iota(jnp.int32, (nsel, nsel * BLOCK), 1) // BLOCK
    broad = (across == lax.broadcasted_iota(jnp.int32, (nsel, nsel * BLOCK), 0)).astype(jnp.bfloat16)
    wide = jnp.dot(coupling.astype(jnp.bfloat16), broad, preferred_element_type=jnp.float32).astype(jnp.bfloat16)
    full = jnp.dot(tall, wide, preferred_element_type=jnp.float32)
    same = (lax.broadcasted_iota(jnp.int32, full.shape, 0) % BLOCK
            == lax.broadcasted_iota(jnp.int32, full.shape, 1) % BLOCK)
    kron_ref[...] = jnp.where(same, full, 0.0).astype(jnp.bfloat16)

    def right(stage, h):
        if 1 <= h < nline:
            if stage is spread_first:
                hop(RIGHT, h)
            stage(RIGHT, h)

    for h in range(1, nline + 2):
        right(spread_first, h)
        if h == 2:
            depart(LEFT)
        if h == 2 and early:
            early_mix()
        if 1 <= h - 2 < nline - 1:
            hop(LEFT, h - 2)
        right(spread_second, h - 1)
        if h == nline:
            for k in range(1, nline - 1):
                spread_first(LEFT, k)
        right(spread_third, h - 2)
    load_r.wait()
    if not early:
        load_a.wait()
    core_whole(RIGHT).wait_recv()
    for h in hops:
        spread_last(RIGHT, h)

    def swap_copy(s, i, f):
        return remote(h_ref.at[s], g_ref.at[s], swap_send.at[s], swap_recv.at[s], pair, place(i, f))

    def half(i, f):
        start = pl.multiple_of(place(i, f) * width, width)
        block = jnp.dot(a_ref[...].reshape(own * rows, cols), r_ref[:, pl.ds(start, width)],
                        preferred_element_type=jnp.float32)
        return block.astype(jnp.bfloat16).reshape(own, npair, strip, width)

    def rotate(s, carry):
        i, f = s // CORES, s % CORES
        h_ref[s] = half(i, f)
        swap_copy(s, i, f).start()
        return carry

    def in_rows(s, position):
        return g_ref.at[s, :, position, pl.ds(early, late), :]

    def in_copy(s, e):
        return remote(in_rows(s, partner(e)), x_ref.at[s, pair], in_send.at[s, e], in_recv.at[s, e], partner(e), mat)

    def in_local(s):
        return pltpu.make_async_copy(in_rows(s, pair), x_ref.at[s, pair], in_recv.at[s, 0])

    def out_rows(s, start, count):
        at = flip(core, s % CORES, CORES) * rows + pair * strip + start
        return z_ref.at[s // CORES, :, pl.ds(pl.multiple_of(at, BLOCK), count), :]

    def pass_copy(s, e):
        return remote(g_ref.at[s, :, partner(e), pl.ds(0, early), :], out_rows(s, 0, early),
                      pass_send.at[s, e], pass_recv.at[s, e], partner(e), mat)

    def pass_local(s):
        return pltpu.make_async_copy(g_ref.at[s, :, pair, pl.ds(0, early), :], out_rows(s, 0, early),
                                     pass_recv.at[s, 0])

    def out_copy(s, e):
        return remote(y_ref.at[s, partner(e)], out_rows(s, early, late), out_send.at[s, e], out_recv.at[s, e],
                      partner(e), mat)

    def out_local(s):
        return pltpu.make_async_copy(y_ref.at[s, pair], out_rows(s, early, late), out_recv.at[s, 0])

    def enter(s):
        if s > 0:
            swap_copy(s, s // CORES, s % CORES).wait_recv()
        for e in peers[::-1]:
            launch(lambda e=e: in_copy(s, e))
        in_local(s).start()
        if early:
            for e in peers[::-1]:
                launch(lambda e=e: pass_copy(s, e))
            pass_local(s).start()

    def mix(s):
        for e in peers:
            in_copy(s, e).wait_recv()
        in_local(s).wait()

        def chunk(b, carry):
            at = pl.ds(pl.multiple_of(b * BLOCK, BLOCK), BLOCK)
            block = x_ref[s, :, :, at, :].reshape(nsel * BLOCK, width)
            mixed = jnp.dot(kron_ref[...], block, preferred_element_type=jnp.float32)
            y_ref[s, :, :, at, :] = mixed.astype(jnp.bfloat16).reshape(npair, ntg, BLOCK, width)
            return carry

        lax.fori_loop(0, late // BLOCK, chunk, 0)
        for e in peers[::-1]:
            launch(lambda e=e: out_copy(s, e))
        out_local(s).start()

    tile = min(512, cols)

    def arrived(s):
        for e in peers:
            out_copy(s, e).wait_recv()
        out_local(s).wait()
        if early:
            for e in peers:
                pass_copy(s, e).wait_recv()
            pass_local(s).wait()

    steps = cols // tile

    def product(i, f, add, last):
        source = flip(line, offset_of(i, nline), nline)
        if f is None:
            depth = pl.ds(0, CORES * rows)
        else:
            depth = pl.ds(pl.multiple_of(flip(core, f, CORES) * rows, rows), rows)

        def target(n, carry):
            t, at = n // steps, pl.ds(pl.multiple_of(n % steps * tile, tile), tile)
            part = jnp.dot(lt_ref[source, at, depth], z_ref[i, t, depth, :], preferred_element_type=jnp.float32)
            if add:
                part = part + acc_ref[t, at, :]
            if last:
                stage_ref[t, at, :] = part.astype(jnp.bfloat16)
            else:
                acc_ref[t, at, :] = part
            return carry

        return target

    def finish(i):
        for f in range(CORES):
            arrived(i * CORES + f)
        lax.fori_loop(0, ntg * steps, product(i, None, i > 0, False), 0)

    def finish_last():
        i = nline - 1
        for f in range(CORES):
            arrived(i * CORES + f)
            if f < CORES - 1:
                lax.fori_loop(0, ntg * steps, product(i, f, i + f > 0, False), 0)
        for t in range(ntg):
            lax.fori_loop(t * steps, (t + 1) * steps, product(i, CORES - 1, True, True), 0)
            pltpu.make_async_copy(stage_ref.at[t], out_hbm.at[t], store_sem.at[t]).start()

    lax.fori_loop(CORES, 2 * CORES, rotate, 0)
    g_ref[0] = half(0, 0)
    enter(0)
    lax.fori_loop(1, CORES, rotate, 0)
    hop(LEFT, nline - 1)
    spread_first(LEFT, nline - 1)
    enter(1)
    lax.fori_loop(2 * CORES, nmat, rotate, 0)

    for i in range(nline):
        first = i * CORES
        if i > 0:
            for f in range(CORES):
                enter(first + f)
        for f in range(CORES):
            mix(first + f)
            if i == 0:
                for h in hops:
                    (spread_second if f == 0 else spread_third)(LEFT, h)
        if i == 1:
            core_whole(LEFT).wait_recv()
            for h in hops:
                spread_last(LEFT, h)
        if i > 0:
            finish(i - 1)
    finish_last()

    for s in range(1, nmat):
        swap_copy(s, s // CORES, s % CORES).wait_send()
    for make, cond in sent:
        if cond is None:
            make().wait_send()
        else:
            pl.when(cond)(lambda make=make: make().wait_send())
    for t in range(ntg):
        pltpu.make_async_copy(stage_ref.at[t], out_hbm.at[t], store_sem.at[t]).wait()


def shards(operators, left_rot, right_rot, integrals, pair_index, target_index):
    npair, nmat = lax.axis_size("pair"), lax.axis_size("mat")
    nline = nmat // CORES
    own, rows, cols = operators.shape
    width = cols // nmat
    strip = rows // npair
    early = early_rows(own, target_index.shape[0] // npair, strip)
    ntgt, nsel = target_index.shape[0], pair_index.shape[0]
    ntg = ntgt // npair
    bf16, f32 = jnp.bfloat16, jnp.float32
    dma = pltpu.SemaphoreType.DMA
    anywhere = pl.BlockSpec(memory_space=pl.ANY)
    scalars = pl.BlockSpec(memory_space=pltpu.SMEM)
    return pl.pallas_call(
        functools.partial(kernel, npair, nline),
        out_shape=jax.ShapeDtypeStruct((ntg, cols, width), bf16),
        in_specs=[scalars, scalars, anywhere, anywhere, anywhere, anywhere],
        out_specs=anywhere,
        scratch_shapes=[
            pltpu.VMEM((own, npair, strip, cols), bf16),
            pltpu.VMEM((npair, own, BLOCK, cols), bf16),
            pltpu.VMEM((cols, cols), bf16),
            pltpu.VMEM((rows, cols), bf16),
            pltpu.VMEM((nline, cols, CORES * rows), bf16),
            pltpu.VMEM(integrals.shape, f32),
            pltpu.VMEM((ntgt, integrals.shape[1]), f32),
            pltpu.VMEM((ntgt * BLOCK, nsel * BLOCK), bf16),
            pltpu.VMEM((nmat, own, npair, strip, width), bf16),
            pltpu.VMEM((nmat, own, npair, strip, width), bf16),
            pltpu.VMEM((nmat, npair, own, strip - early, width), bf16),
            pltpu.VMEM((nmat, npair, ntg, strip - early, width), bf16),
            pltpu.VMEM((nline, ntg, CORES * rows, width), bf16),
            pltpu.VMEM((ntg, cols, width), f32),
            pltpu.VMEM((ntg, cols, width), bf16),
            dma((4,)),
            dma((2, nline, 2)), dma((2, nline)),
            dma((2, nline, npair, 2)), dma((2, nline, npair, 2)),
            dma((2, nline, npair)), dma((2, nline, npair)),
            dma((nmat,)), dma((nmat,)),
            dma((npair,)), dma((npair,)),
            dma((nmat, npair)), dma((nmat, npair)),
            dma((nmat, npair)), dma((nmat, npair)),
            dma((nmat, npair)), dma((nmat, npair)),
            dma((ntg,)),
        ],
        compiler_params=pltpu.CompilerParams(
            collective_id=0, has_side_effects=True, vmem_limit_bytes=67043328),
    )(target_index, pair_index, operators.reshape(own, npair, strip, cols), right_rot, left_rot, integrals)


def solution(mesh):
    in_specs = (P("pair", "mat", None), P("mat", None), P("mat", None), P(), P(), P())
    out_specs = P("pair", None, "mat")
    return jax.shard_map(shards, mesh=mesh, in_specs=in_specs, out_specs=out_specs, check_vma=False)
```

```python
import functools

import jax
import jax.numpy as jnp
from jax import lax
from jax.experimental import pallas as pl
from jax.experimental.pallas import tpu as pltpu
from jax.sharding import PartitionSpec as P

CORES = 2
NEAR = 2
BLOCK = 16
LEFT = 2
UP, DOWN = 0, 1
MESH_ID = pl.DeviceIdType.MESH


def flip(index, offset, count):
    total, bit = 0, 1
    while bit < count:
        total = total + bit * ((index // bit + offset // bit) % 2)
        bit *= 2
    return total


def offset_of(i, nline):
    if isinstance(i, int):
        return 0 if i == 0 else (nline - 1 - (i - 1) // 2 if i % 2 == 1 else i // 2)
    odd = i % 2
    return odd * (nline - 1 - (i - 1) // 2) + (1 - odd) * (i // 2)


def early_rows(own, ntg, strip):
    return BLOCK if own == ntg and strip > BLOCK else 0


def kernel(npair, nline, targets_ref, pairs_ref, a_hbm, r_hbm, l_hbm, integrals_hbm, stage_ref,
           a_ref, early_ref, r_ref, l_ref, lt_ref, integrals_ref, rows_ref, kron_ref, h_ref, g_ref, x_ref, y_ref, z_ref,
           acc_ref,
           load_sem, line_send, line_recv, plane_send, plane_recv, core_send, core_recv, whole_send, whole_recv,
           swap_send, swap_recv, first_send, first_recv, in_send, in_recv, pass_send, out_send, out_recv):
    own, _, strip, cols = a_hbm.shape
    rows = npair * strip
    ntgt, nsel = targets_ref.shape[0], pairs_ref.shape[0]
    ntg = ntgt // npair
    nmat = nline * CORES
    width = cols // nmat
    early = early_rows(own, ntg, strip)
    late = strip - early
    mpiece = cols // npair
    pair, mat = lax.axis_index("pair"), lax.axis_index("mat")
    line, core = mat // CORES, mat % CORES
    peers = tuple(range(1, npair))
    straight = tuple(e for e in peers if e % NEAR == 0 or e // NEAR == 0)
    far = tuple(e for e in peers if e not in straight)
    hops = range(1, nline)

    def place(i, f):
        return flip(line, offset_of(i, nline), nline) * CORES + flip(core, f, CORES)

    def partner(e):
        return flip(pair, e, npair)

    sibling = line * CORES + flip(core, 1, CORES)

    def remote(src, dst, send, recv, pair_id, mat_id):
        return pltpu.make_async_remote_copy(
            src_ref=src, dst_ref=dst, send_sem=send, recv_sem=recv,
            device_id={"pair": pair_id, "mat": mat_id}, device_id_type=MESH_ID)

    def launch(make, cond=None):
        if cond is None:
            make().start()
        else:
            pl.when(cond)(lambda: make().start())

    def await_bytes(block, sem):
        pltpu.make_async_copy(block, block, sem).wait()

    chained = []

    load_r = pltpu.make_async_copy(r_hbm, r_ref.at[pl.ds(pl.multiple_of(mat * rows, rows), rows), :], load_sem.at[0])
    load_l = pltpu.make_async_copy(l_hbm, l_ref, load_sem.at[1])
    load_i = pltpu.make_async_copy(integrals_hbm, integrals_ref, load_sem.at[2])
    load_a = pltpu.make_async_copy(a_hbm, a_ref, load_sem.at[3])
    for copy in (load_l, load_i, load_r, load_a):
        copy.start()

    barrier = pltpu.get_barrier_semaphore()
    for s in range(1, nmat):
        pl.semaphore_signal(barrier, inc=1, device_id={"pair": pair, "mat": place(s // CORES, s % CORES)},
                            device_id_type=MESH_ID)
    for e in peers:
        pl.semaphore_signal(barrier, inc=1, device_id={"pair": partner(e), "mat": mat}, device_id_type=MESH_ID)
    pl.semaphore_wait(barrier, nmat - 1 + len(peers))

    def piece(m, source, c, origin, part=None):
        if m is not LEFT:
            at = pl.multiple_of((source * CORES + c) * rows + origin * strip, strip)
            size = cols // 2 if part is None else cols // 4
            start = m * (cols // 2) + (0 if part is None else part * size)
            return r_ref.at[pl.ds(at, strip), pl.ds(pl.multiple_of(start, size), size)]
        lanes = pl.ds(pl.multiple_of(c * rows, rows), rows)
        at = pl.multiple_of(origin * mpiece, mpiece)
        if part is None:
            return lt_ref.at[source, pl.ds(at, mpiece), lanes]
        at = pl.multiple_of(at + part * (mpiece // 2), mpiece // 2)
        return lt_ref.at[source, pl.ds(at, mpiece // 2), lanes]

    def own_piece(m):
        if m is not LEFT:
            return r_hbm.at[pl.ds(pl.multiple_of(pair * strip, strip), strip), pl.ds(m * (cols // 2), cols // 2)]
        return piece(LEFT, line, core, pair)

    def chain_copy(m, source, way, first):
        block = piece(m, source, core, pair)
        step = 1 if way == UP else -1
        return remote(own_piece(m) if first else block, block, line_send.at[m, source, way], line_recv.at[m, source],
                      pair, (line + step) * CORES + core)

    def line_arrival(m, source):
        block = piece(m, source, core, pair)
        return remote(block, block, line_send.at[m, source, UP], line_recv.at[m, source], pair, sibling)

    def plane_copy(m, source, to, origin, part=None):
        block = piece(m, source, core, partner(origin), part)
        k = to ^ origin
        return remote(block, block, plane_send.at[m], plane_recv.at[m, source, k], partner(to), mat)

    def plane_arrival(m, source, e):
        block = piece(m, source, core, partner(e))
        return remote(block, block, plane_send.at[m], plane_recv.at[m, source, e], partner(e), mat)

    def core_copy(m, source, e):
        block = piece(m, source, core, partner(e))
        return remote(block, block, core_send.at[m], core_recv.at[m], pair, sibling)

    def core_whole(m):
        if m is not LEFT:
            src, dst = r_hbm, r_ref.at[pl.ds(pl.multiple_of(mat * rows, rows), rows), :]
        else:
            src = dst = lt_ref.at[line, :, pl.ds(pl.multiple_of(core * rows, rows), rows)]
        k = 1 if m is LEFT else 0
        return remote(src, dst, whole_send.at[k], whole_recv.at[k], pair, sibling)

    def reaches(way, h):
        if way == UP:
            return line >= h, line - h
        return line + h < nline, line + h

    def both(h, act):
        for way in (UP, DOWN):
            cond, source = reaches(way, h)
            act(way, cond, source)

    def chain(make, cond):
        chained.append((make, cond))
        launch(make, cond)

    def hop(m, h, ways=(UP, DOWN)):
        for way in ways:
            cond, source = reaches(way, h)
            pl.when(cond)(lambda: line_arrival(m, source).wait_recv())
            if h + 1 < nline:
                more = line < nline - 1 if way == UP else line > 0
                chain(lambda m=m, source=source, way=way: chain_copy(m, source, way, False), cond & more)

    def spread_way(m, way, cond, source):
        for e in straight:
            launch(lambda e=e: plane_copy(m, source, e, 0), cond)
        launch(lambda: core_copy(m, source, 0), cond)

    def spread_first(m, h):
        both(h, lambda way, cond, source: spread_way(m, way, cond, source))

    def spread_second(m, h):
        def act(way, cond, source):
            for e in straight:
                pl.when(cond)(lambda e=e: plane_arrival(m, source, e).wait_recv())
                for to in straight:
                    if to ^ e in far:
                        launch(lambda e=e, to=to: plane_copy(m, source, to, e, 0 if e < NEAR else 1), cond)
                launch(lambda e=e: core_copy(m, source, e), cond)
        both(h, act)

    def spread_third(m, h):
        def act(way, cond, source):
            for e in far:
                pl.when(cond)(lambda e=e: plane_arrival(m, source, e).wait_recv())
                launch(lambda e=e: core_copy(m, source, e), cond)
        both(h, act)

    def gathered(m):
        if m is not LEFT:
            return r_ref.at[pl.ds(0, (nline - 1) * rows), pl.ds(0, cols // 2)]
        return lt_ref.at[pl.ds(0, nline - 1), :, pl.ds(0, rows)]

    def spread_last(m):
        await_bytes(gathered(m), core_recv.at[m])

    def depart(m, way):
        chain(lambda: chain_copy(m, line, way, True), line < nline - 1 if way == UP else line > 0)

    def early_source(position):
        return a_hbm.at[:, position, pl.ds(0, early), :]

    def early_copy(e):
        return remote(early_source(partner(e)), early_ref.at[pair], first_send.at[0], first_recv.at[0],
                      partner(e), mat)

    def early_mix():
        await_bytes(early_ref, first_recv.at[0])
        load_a.wait()
        span = min(512, cols)

        def columns(b, carry):
            at = pl.ds(pl.multiple_of(b * span, span), span)
            mixed = jnp.dot(kron_ref[...], early_ref[:, :, :, at].reshape(nsel * BLOCK, span),
                            preferred_element_type=jnp.float32)
            mixed = mixed.astype(jnp.bfloat16).reshape(npair, ntg, BLOCK, span)
            for position in range(npair):
                a_ref[:, position, pl.ds(0, early), at] = mixed[position]
            return carry

        lax.fori_loop(0, cols // span, columns, 0)

    for turn_of in range(2):
        depart(turn_of, UP)
        depart(1 - turn_of, DOWN)
    launch(lambda: core_whole(0))
    if early:
        for e in peers[::-1]:
            launch(lambda e=e: early_copy(e))
        pltpu.make_async_copy(early_source(pair), early_ref.at[pair], first_recv.at[0]).start()

    load_l.wait()
    lanes = pl.ds(pl.multiple_of(core * rows, rows), rows)

    def turn(b, carry):
        at = pl.ds(pl.multiple_of(b * 256, 256), 256)
        lt_ref[line, at, lanes] = l_ref[:, at].T
        return carry

    lax.fori_loop(0, cols // 256, turn, 0)

    load_i.wait()
    for t in range(ntgt):
        rows_ref[pl.ds(t, 1), :] = integrals_ref[pl.ds(targets_ref[t], 1), :]
    picked = rows_ref[...]
    lane = lax.broadcasted_iota(jnp.int32, picked.shape, 1)
    column = lax.broadcasted_iota(jnp.int32, (ntgt, nsel), 1)
    coupling = jnp.zeros((ntgt, nsel), jnp.float32)
    for k in range(nsel):
        value = jnp.sum(jnp.where(lane == pairs_ref[k], picked, 0.0), axis=1, keepdims=True)
        coupling = jnp.where(column == k, value, coupling)
    down = lax.broadcasted_iota(jnp.int32, (ntgt * BLOCK, ntgt), 0) // BLOCK
    tall = (down == lax.broadcasted_iota(jnp.int32, (ntgt * BLOCK, ntgt), 1)).astype(jnp.bfloat16)
    across = lax.broadcasted_iota(jnp.int32, (nsel, nsel * BLOCK), 1) // BLOCK
    broad = (across == lax.broadcasted_iota(jnp.int32, (nsel, nsel * BLOCK), 0)).astype(jnp.bfloat16)
    wide = jnp.dot(coupling.astype(jnp.bfloat16), broad, preferred_element_type=jnp.float32).astype(jnp.bfloat16)
    full = jnp.dot(tall, wide, preferred_element_type=jnp.float32)
    same = (lax.broadcasted_iota(jnp.int32, full.shape, 0) % BLOCK
            == lax.broadcasted_iota(jnp.int32, full.shape, 1) % BLOCK)
    kron_ref[...] = jnp.where(same, full, 0.0).astype(jnp.bfloat16)

    near = line // (nline // 2)
    away = 1 - near

    def hop_right(h):
        for turn_of in range(2):
            for way, m in ((UP, turn_of), (DOWN, 1 - turn_of)):
                hop(m, h, (way,))
                cond, source = reaches(way, h)
                spread_way(m, way, cond & (away == m), source)

    for h in hops:
        hop_right(h)
        if h == max(1, nline - 2):
            depart(LEFT, UP)
            depart(LEFT, DOWN)
            launch(lambda: core_whole(LEFT))
            if early:
                early_mix()
        if h > 1:
            spread_second(away, h - 1)
        if h == nline - 1 and nline > 2:
            hop(LEFT, 1)
    spread_second(away, nline - 1)
    for h in hops:
        spread_first(near, h)
    for h in hops:
        spread_third(away, h)
    load_r.wait()
    if not early:
        load_a.wait()
    for h in range(2, nline - 1):
        hop(LEFT, h)
    core_whole(0).wait_recv()
    spread_last(away)

    def swap_copy(s, i, f):
        return remote(h_ref.at[s], g_ref.at[s], swap_send.at[0], swap_recv.at[s], pair, place(i, f))

    def half(i, f):
        start = pl.multiple_of(place(i, f) * width, width)
        block = jnp.dot(a_ref[...].reshape(own * rows, cols), r_ref[:, pl.ds(start, width)],
                        preferred_element_type=jnp.float32)
        return block.astype(jnp.bfloat16).reshape(own, npair, strip, width)

    def rotate(s, carry):
        i, f = s // CORES, s % CORES
        h_ref[s] = half(i, f)
        swap_copy(s, i, f).start()
        return carry

    def in_rows(s, position):
        return g_ref.at[s, :, position, pl.ds(early, late), :]

    def in_copy(s, e):
        return remote(in_rows(s, partner(e)), x_ref.at[s, pair], in_send.at[0], in_recv.at[s], partner(e), mat)

    def in_local(s):
        return pltpu.make_async_copy(in_rows(s, pair), x_ref.at[s, pair], in_recv.at[s])

    def out_rows(s, start, count):
        at = flip(core, s % CORES, CORES) * rows + pair * strip + start
        return z_ref.at[s // CORES, :, pl.ds(pl.multiple_of(at, BLOCK), count), :]

    def pass_copy(s, e):
        return remote(g_ref.at[s, :, partner(e), pl.ds(0, early), :], out_rows(s, 0, early),
                      pass_send.at[0], out_recv.at[s], partner(e), mat)

    def pass_local(s):
        return pltpu.make_async_copy(g_ref.at[s, :, pair, pl.ds(0, early), :], out_rows(s, 0, early),
                                     out_recv.at[s])

    def out_copy(s, e):
        return remote(y_ref.at[s, partner(e)], out_rows(s, early, late), out_send.at[0], out_recv.at[s],
                      partner(e), mat)

    def out_local(s):
        return pltpu.make_async_copy(y_ref.at[s, pair], out_rows(s, early, late), out_recv.at[s])

    def enter(s):
        if s > 0:
            swap_copy(s, s // CORES, s % CORES).wait_recv()
        for e in peers[::-1]:
            launch(lambda e=e: in_copy(s, e))
        in_local(s).start()
        if early:
            for e in peers[::-1]:
                launch(lambda e=e: pass_copy(s, e))
            pass_local(s).start()

    def mix(s):
        await_bytes(x_ref.at[s], in_recv.at[s])

        def chunk(b, carry):
            at = pl.ds(pl.multiple_of(b * BLOCK, BLOCK), BLOCK)
            block = x_ref[s, :, :, at, :].reshape(nsel * BLOCK, width)
            mixed = jnp.dot(kron_ref[...], block, preferred_element_type=jnp.float32)
            y_ref[s, :, :, at, :] = mixed.astype(jnp.bfloat16).reshape(npair, ntg, BLOCK, width)
            return carry

        lax.fori_loop(0, late // BLOCK, chunk, 0)
        for e in peers[::-1]:
            launch(lambda e=e: out_copy(s, e))
        out_local(s).start()

    tile = min(512, cols)

    def arrived(s):
        await_bytes(z_ref.at[s // CORES, :, pl.ds(0, rows), :], out_recv.at[s])

    steps = cols // tile

    def product(i, f, add, last):
        source = flip(line, offset_of(i, nline), nline)
        if f is None:
            depth = pl.ds(0, CORES * rows)
        else:
            depth = pl.ds(pl.multiple_of(flip(core, f, CORES) * rows, rows), rows)

        def target(n, carry):
            t, at = n // steps, pl.ds(pl.multiple_of(n % steps * tile, tile), tile)
            part = jnp.dot(lt_ref[source, at, depth], z_ref[i, t, depth, :], preferred_element_type=jnp.float32)
            if add:
                part = part + acc_ref[t, at, :]
            if last:
                stage_ref[t, at, :] = part.astype(jnp.bfloat16)
            else:
                acc_ref[t, at, :] = part
            return carry

        return target

    def finish(i):
        for f in range(CORES):
            arrived(i * CORES + f)
        lax.fori_loop(0, ntg * steps, product(i, None, i > 0, False), 0)

    def finish_last():
        i = nline - 1
        for f in range(CORES):
            arrived(i * CORES + f)
            if f < CORES - 1:
                lax.fori_loop(0, ntg * steps, product(i, f, i + f > 0, False), 0)
        for t in range(ntg):
            lax.fori_loop(t * steps, (t + 1) * steps, product(i, CORES - 1, True, True), 0)

    lax.fori_loop(CORES, 2 * CORES, rotate, 0)
    for h in hops:
        spread_second(near, h)
    for h in range(1, nline - 1):
        spread_first(LEFT, h)
    for h in hops:
        spread_third(near, h)
    spread_last(near)
    g_ref[0] = half(0, 0)
    enter(0)
    lax.fori_loop(1, CORES, rotate, 0)
    enter(1)
    lax.fori_loop(2 * CORES, nmat, rotate, 0)

    for i in range(nline):
        first = i * CORES
        if i > 0:
            for f in range(CORES):
                enter(first + f)
        for f in range(CORES):
            mix(first + f)
            stage = i * CORES + f
            last = nline - 1
            if stage == 0:
                for h in range(1, last):
                    spread_second(LEFT, h)
                hop(LEFT, last)
                spread_first(LEFT, last)
            if stage == 1:
                for h in range(1, last):
                    spread_third(LEFT, h)
            if stage == 2:
                spread_second(LEFT, last)
            if stage == min(4, nmat - 1):
                spread_third(LEFT, last)
            if i > 0 and f == 0:
                if i == 1:
                    core_whole(LEFT).wait_recv()
                if i == min(2, nline - 1):
                    spread_last(LEFT)
                finish(i - 1)
    finish_last()

    count = (nline - 1) * (npair - 1)
    for m in range(2):
        await_bytes(r_ref.at[pl.ds(0, count * strip), pl.ds(0, cols // 2)], plane_send.at[m])
    await_bytes(lt_ref.at[pl.ds(0, nline - 1), pl.ds(0, (npair - 1) * mpiece), pl.ds(0, rows)], plane_send.at[LEFT])
    for m in range(LEFT + 1):
        await_bytes(gathered(m), core_send.at[m])
    for m in (0, LEFT):
        core_whole(m).wait_send()
    await_bytes(h_ref.at[pl.ds(1, nmat - 1)], swap_send.at[0])
    await_bytes(x_ref.at[:, pl.ds(0, npair - 1)], in_send.at[0])
    await_bytes(y_ref.at[:, pl.ds(0, npair - 1)], out_send.at[0])
    if early:
        await_bytes(early_ref.at[pl.ds(0, npair - 1)], first_send.at[0])
        await_bytes(g_ref.at[:, :, pl.ds(0, npair - 1), pl.ds(0, early), :], pass_send.at[0])
    for make, cond in chained:
        pl.when(cond)(lambda make=make: make().wait_send())


def shards(operators, left_rot, right_rot, integrals, pair_index, target_index):
    npair, nmat = lax.axis_size("pair"), lax.axis_size("mat")
    nline = nmat // CORES
    own, rows, cols = operators.shape
    width = cols // nmat
    strip = rows // npair
    early = early_rows(own, target_index.shape[0] // npair, strip)
    ntgt, nsel = target_index.shape[0], pair_index.shape[0]
    ntg = ntgt // npair
    bf16, f32 = jnp.bfloat16, jnp.float32
    dma = pltpu.SemaphoreType.DMA
    anywhere = pl.BlockSpec(memory_space=pl.ANY)
    scalars = pl.BlockSpec(memory_space=pltpu.SMEM)
    return pl.pallas_call(
        functools.partial(kernel, npair, nline),
        out_shape=pltpu.VMEM((ntg, cols, width), bf16),
        in_specs=[scalars, scalars, anywhere, anywhere, anywhere, anywhere],
        out_specs=pl.BlockSpec(memory_space=pltpu.VMEM),
        scratch_shapes=[
            pltpu.VMEM((own, npair, strip, cols), bf16),
            pltpu.VMEM((npair, own, BLOCK, cols), bf16),
            pltpu.VMEM((cols, cols), bf16),
            pltpu.VMEM((rows, cols), bf16),
            pltpu.VMEM((nline, cols, CORES * rows), bf16),
            pltpu.VMEM(integrals.shape, f32),
            pltpu.VMEM((ntgt, integrals.shape[1]), f32),
            pltpu.VMEM((ntgt * BLOCK, nsel * BLOCK), bf16),
            pltpu.VMEM((nmat, own, npair, strip, width), bf16),
            pltpu.VMEM((nmat, own, npair, strip, width), bf16),
            pltpu.VMEM((nmat, npair, own, strip - early, width), bf16),
            pltpu.VMEM((nmat, npair, ntg, strip - early, width), bf16),
            pltpu.VMEM((nline, ntg, CORES * rows, width), bf16),
            pltpu.VMEM((ntg, cols, width), f32),
            dma((4,)),
            dma((3, nline, 2)), dma((3, nline)),
            dma((3,)), dma((3, nline, npair)),
            dma((3,)), dma((3,)), dma((2,)), dma((2,)),
            dma((1,)), dma((nmat,)),
            dma((1,)), dma((1,)),
            dma((1,)), dma((nmat,)),
            dma((1,)), dma((1,)), dma((nmat,)),
        ],
        compiler_params=pltpu.CompilerParams(
            collective_id=0, has_side_effects=True, vmem_limit_bytes=56623104),
    )(target_index, pair_index, operators.reshape(own, npair, strip, cols), right_rot, left_rot, integrals)


def solution(mesh):
    in_specs = (P("pair", "mat", None), P("mat", None), P("mat", None), P(), P(), P())
    out_specs = P("pair", None, "mat")
    return jax.shard_map(shards, mesh=mesh, in_specs=in_specs, out_specs=out_specs, check_vma=False)
```

```python
import functools

import jax
import jax.numpy as jnp
from jax import lax
from jax.experimental import pallas as pl
from jax.experimental.pallas import tpu as pltpu
from jax.sharding import PartitionSpec as P

CORES = 2
NEAR = 2
BLOCK = 16
BESIDE = 3
LEFT = 2
UP, DOWN = 0, 1
MESH_ID = pl.DeviceIdType.MESH


def flip(index, offset, count):
    total, bit = 0, 1
    while bit < count:
        total = total + bit * ((index // bit + offset // bit) % 2)
        bit *= 2
    return total


def offset_of(i, nline):
    if isinstance(i, int):
        return 0 if i == 0 else (nline - 1 - (i - 1) // 2 if i % 2 == 1 else i // 2)
    odd = i % 2
    return odd * (nline - 1 - (i - 1) // 2) + (1 - odd) * (i // 2)


def early_rows(own, ntg, strip):
    return BLOCK if own == ntg and strip > BLOCK else 0


def kernel(npair, nline, targets_ref, pairs_ref, a_hbm, r_hbm, l_hbm, integrals_hbm, stage_ref,
           a_ref, early_ref, r_ref, l_ref, lt_ref, integrals_ref, rows_ref, kron_ref, h_ref, g_ref, x_ref, y_ref, z_ref,
           acc_ref,
           load_sem, line_send, line_recv, plane_send, plane_recv, core_send, core_recv, whole_send, whole_recv,
           next_send, next_recv,
           swap_send, swap_recv, first_send, first_recv, in_send, in_recv, pass_send, out_send, out_recv):
    own, _, strip, cols = a_hbm.shape
    rows = npair * strip
    ntgt, nsel = targets_ref.shape[0], pairs_ref.shape[0]
    ntg = ntgt // npair
    nmat = nline * CORES
    width = cols // nmat
    early = early_rows(own, ntg, strip)
    late = strip - early
    mpiece = cols // npair
    pair, mat = lax.axis_index("pair"), lax.axis_index("mat")
    line, core = mat // CORES, mat % CORES
    peers = tuple(range(1, npair))
    straight = tuple(e for e in peers if e % NEAR == 0 or e // NEAR == 0)
    far = tuple(e for e in peers if e not in straight)
    hops = range(1, nline)

    def place(i, f):
        return flip(line, offset_of(i, nline), nline) * CORES + flip(core, f, CORES)

    def partner(e):
        return flip(pair, e, npair)

    sibling = line * CORES + flip(core, 1, CORES)

    def remote(src, dst, send, recv, pair_id, mat_id):
        return pltpu.make_async_remote_copy(
            src_ref=src, dst_ref=dst, send_sem=send, recv_sem=recv,
            device_id={"pair": pair_id, "mat": mat_id}, device_id_type=MESH_ID)

    def launch(make, cond=None):
        if cond is None:
            make().start()
        else:
            pl.when(cond)(lambda: make().start())

    def await_bytes(block, sem):
        pltpu.make_async_copy(block, block, sem).wait()

    chained = []

    load_r = pltpu.make_async_copy(r_hbm, r_ref.at[pl.ds(pl.multiple_of(mat * rows, rows), rows), :], load_sem.at[0])
    load_l = pltpu.make_async_copy(l_hbm, l_ref, load_sem.at[1])
    load_i = pltpu.make_async_copy(integrals_hbm, integrals_ref, load_sem.at[2])
    load_a = pltpu.make_async_copy(a_hbm, a_ref, load_sem.at[3])
    for copy in (load_l, load_i, load_r, load_a):
        copy.start()

    barrier = pltpu.get_barrier_semaphore()
    for s in range(1, nmat):
        pl.semaphore_signal(barrier, inc=1, device_id={"pair": pair, "mat": place(s // CORES, s % CORES)},
                            device_id_type=MESH_ID)
    for e in peers:
        pl.semaphore_signal(barrier, inc=1, device_id={"pair": partner(e), "mat": mat}, device_id_type=MESH_ID)
    pl.semaphore_wait(barrier, nmat - 1 + len(peers))

    def piece(m, source, c, origin, part=None):
        if m is not LEFT:
            at = pl.multiple_of((source * CORES + c) * rows + origin * strip, strip)
            size = cols // 2 if part is None else cols // 4
            start = m * (cols // 2) + (0 if part is None else part * size)
            return r_ref.at[pl.ds(at, strip), pl.ds(pl.multiple_of(start, size), size)]
        lanes = pl.ds(pl.multiple_of(c * rows, rows), rows)
        at = pl.multiple_of(origin * mpiece, mpiece)
        if part is None:
            return lt_ref.at[source, pl.ds(at, mpiece), lanes]
        at = pl.multiple_of(at + part * (mpiece // 2), mpiece // 2)
        return lt_ref.at[source, pl.ds(at, mpiece // 2), lanes]

    def own_piece(m):
        if m is not LEFT:
            return r_hbm.at[pl.ds(pl.multiple_of(pair * strip, strip), strip), pl.ds(m * (cols // 2), cols // 2)]
        return piece(LEFT, line, core, pair)

    def chain_copy(m, source, way, first):
        block = piece(m, source, core, pair)
        step = 1 if way == UP else -1
        return remote(own_piece(m) if first else block, block, line_send.at[m, source, way], line_recv.at[m, source],
                      pair, (line + step) * CORES + core)

    def line_arrival(m, source):
        block = piece(m, source, core, pair)
        return remote(block, block, line_send.at[m, source, UP], line_recv.at[m, source], pair, sibling)

    def plane_copy(m, source, to, origin, part=None):
        block = piece(m, source, core, partner(origin), part)
        k = to ^ origin
        return remote(block, block, plane_send.at[m], plane_recv.at[m, source, k], partner(to), mat)

    def plane_arrival(m, source, e):
        block = piece(m, source, core, partner(e))
        return remote(block, block, plane_send.at[m], plane_recv.at[m, source, e], partner(e), mat)

    def core_copy(m, source, e, group=None):
        block = piece(m, source, core, partner(e))
        k = m if group is None else group
        return remote(block, block, core_send.at[k], core_recv.at[k], pair, sibling)

    def core_whole(m):
        if m is not LEFT:
            src, dst = r_hbm, r_ref.at[pl.ds(pl.multiple_of(mat * rows, rows), rows), :]
        else:
            src = dst = lt_ref.at[line, :, pl.ds(pl.multiple_of(core * rows, rows), rows)]
        k = 1 if m is LEFT else 0
        return remote(src, dst, whole_send.at[k], whole_recv.at[k], pair, sibling)

    def reaches(way, h):
        if way == UP:
            return line >= h, line - h
        return line + h < nline, line + h

    def both(h, act):
        for way in (UP, DOWN):
            cond, source = reaches(way, h)
            act(way, cond, source)

    def chain(make, cond):
        chained.append((make, cond))
        launch(make, cond)

    def hop(m, h, ways=(UP, DOWN)):
        for way in ways:
            cond, source = reaches(way, h)
            pl.when(cond)(lambda: line_arrival(m, source).wait_recv())
            if h + 1 < nline:
                more = line < nline - 1 if way == UP else line > 0
                chain(lambda m=m, source=source, way=way: chain_copy(m, source, way, False), cond & more)

    def left_hop(h):
        if h + 1 < nline:
            for way in (UP, DOWN):
                cond, source = reaches(way, h)
                more = cond & (line < nline - 1 if way == UP else line > 0)
                pl.when(more)(lambda: line_arrival(LEFT, source).wait_recv())
                chain(lambda source=source, way=way: chain_copy(LEFT, source, way, False), more)

    def spread_way(m, way, cond, source):
        for e in straight:
            launch(lambda e=e: plane_copy(m, source, e, 0), cond)
        launch(lambda: core_copy(m, source, 0), cond)

    def spread_first(m, h):
        both(h, lambda way, cond, source: spread_way(m, way, cond, source))

    beside = flip(line, 1, nline)

    def next_copy(e):
        block = piece(LEFT, line, core, partner(e))
        return remote(block, block, next_send.at[0], next_recv.at[0], pair, beside * CORES + core)

    def left_first(h):
        def act(way, cond, source):
            ends = cond if h + 1 == nline else cond & (line == (nline - 1 if way == UP else 0))
            pl.when(ends)(lambda: line_arrival(LEFT, source).wait_recv())
            if h == 1:
                through = cond & (line % 2 == (0 if way == UP else 1))
                launch(lambda: core_copy(LEFT, source, 0, BESIDE), cond & (line % 2 == (1 if way == UP else 0)))
            else:
                through = cond
            spread_way(LEFT, way, through, source)
        both(h, act)

    def left_beside():
        await_bytes(lt_ref.at[0, pl.ds(0, (npair - 1) * mpiece), pl.ds(0, rows)], next_recv.at[0])
        for e in peers:
            launch(lambda e=e: core_copy(LEFT, beside, e, BESIDE))

    def spread_second(m, h):
        def act(way, cond, source):
            if m is LEFT and h == 1:
                cond = cond & (line % 2 == (0 if way == UP else 1))
            for e in straight:
                pl.when(cond)(lambda e=e: plane_arrival(m, source, e).wait_recv())
                for to in straight:
                    if to ^ e in far:
                        launch(lambda e=e, to=to: plane_copy(m, source, to, e, 0 if e < NEAR else 1), cond)
                launch(lambda e=e: core_copy(m, source, e), cond)
        both(h, act)

    def spread_third(m, h):
        def act(way, cond, source):
            if m is LEFT and h == 1:
                cond = cond & (line % 2 == (0 if way == UP else 1))
            for e in far:
                pl.when(cond)(lambda e=e: plane_arrival(m, source, e).wait_recv())
                launch(lambda e=e: core_copy(m, source, e), cond)
        both(h, act)

    def gathered(m):
        if m is BESIDE:
            return lt_ref.at[0, :, pl.ds(0, rows)]
        if m is LEFT:
            return lt_ref.at[pl.ds(0, nline - 2), :, pl.ds(0, rows)]
        return r_ref.at[pl.ds(0, (nline - 1) * rows), pl.ds(0, cols // 2)]

    def spread_last(m):
        if m is not LEFT or nline > 2:
            await_bytes(gathered(m), core_recv.at[m])

    def depart(m, way):
        chain(lambda: chain_copy(m, line, way, True), line < nline - 1 if way == UP else line > 0)

    def early_source(position):
        return a_hbm.at[:, position, pl.ds(0, early), :]

    def early_copy(e):
        return remote(early_source(partner(e)), early_ref.at[pair], first_send.at[0], first_recv.at[0],
                      partner(e), mat)

    def early_mix():
        await_bytes(early_ref, first_recv.at[0])
        load_a.wait()
        span = min(512, cols)

        def columns(b, carry):
            at = pl.ds(pl.multiple_of(b * span, span), span)
            mixed = jnp.dot(kron_ref[...], early_ref[:, :, :, at].reshape(nsel * BLOCK, span),
                            preferred_element_type=jnp.float32)
            mixed = mixed.astype(jnp.bfloat16).reshape(npair, ntg, BLOCK, span)
            for position in range(npair):
                a_ref[:, position, pl.ds(0, early), at] = mixed[position]
            return carry

        lax.fori_loop(0, cols // span, columns, 0)

    for turn_of in range(2):
        depart(turn_of, UP)
        depart(1 - turn_of, DOWN)
    launch(lambda: core_whole(0))
    if early:
        for e in peers[::-1]:
            launch(lambda e=e: early_copy(e))
        pltpu.make_async_copy(early_source(pair), early_ref.at[pair], first_recv.at[0]).start()

    load_l.wait()
    lanes = pl.ds(pl.multiple_of(core * rows, rows), rows)

    def turn(b, carry):
        at = pl.ds(pl.multiple_of(b * 256, 256), 256)
        lt_ref[line, at, lanes] = l_ref[:, at].T
        return carry

    lax.fori_loop(0, cols // 256, turn, 0)

    load_i.wait()
    for t in range(ntgt):
        rows_ref[pl.ds(t, 1), :] = integrals_ref[pl.ds(targets_ref[t], 1), :]
    picked = rows_ref[...]
    lane = lax.broadcasted_iota(jnp.int32, picked.shape, 1)
    column = lax.broadcasted_iota(jnp.int32, (ntgt, nsel), 1)
    coupling = jnp.zeros((ntgt, nsel), jnp.float32)
    for k in range(nsel):
        value = jnp.sum(jnp.where(lane == pairs_ref[k], picked, 0.0), axis=1, keepdims=True)
        coupling = jnp.where(column == k, value, coupling)
    down = lax.broadcasted_iota(jnp.int32, (ntgt * BLOCK, ntgt), 0) // BLOCK
    tall = (down == lax.broadcasted_iota(jnp.int32, (ntgt * BLOCK, ntgt), 1)).astype(jnp.bfloat16)
    across = lax.broadcasted_iota(jnp.int32, (nsel, nsel * BLOCK), 1) // BLOCK
    broad = (across == lax.broadcasted_iota(jnp.int32, (nsel, nsel * BLOCK), 0)).astype(jnp.bfloat16)
    wide = jnp.dot(coupling.astype(jnp.bfloat16), broad, preferred_element_type=jnp.float32).astype(jnp.bfloat16)
    full = jnp.dot(tall, wide, preferred_element_type=jnp.float32)
    same = (lax.broadcasted_iota(jnp.int32, full.shape, 0) % BLOCK
            == lax.broadcasted_iota(jnp.int32, full.shape, 1) % BLOCK)
    kron_ref[...] = jnp.where(same, full, 0.0).astype(jnp.bfloat16)

    near = line // (nline // 2)
    away = 1 - near

    def hop_right(h, turn_of):
        for way, m in ((UP, turn_of), (DOWN, 1 - turn_of)):
            hop(m, h, (way,))
            cond, source = reaches(way, h)
            spread_way(m, way, cond & (away == m), source)

    for h in range(1, nline - 1):
        hop_right(h, 0)
        hop_right(h, 1)
    depart(LEFT, UP)
    depart(LEFT, DOWN)
    launch(lambda: core_whole(LEFT))
    hop_right(nline - 1, 0)
    if early:
        early_mix()
    for h in range(1, nline - 1):
        spread_second(away, h)
    left_hop(1)
    spread_second(away, nline - 1)
    hop_right(nline - 1, 1)
    for h in hops:
        spread_first(near, h)
    for h in hops:
        spread_third(away, h)
    load_r.wait()
    if not early:
        load_a.wait()
    core_whole(0).wait_recv()
    spread_last(away)

    def swap_copy(s, i, f, e):
        strips = partner(e)
        return remote(h_ref.at[s, :, strips], g_ref.at[s, :, strips], swap_send.at[0], swap_recv.at[s, e],
                      pair, place(i, f))

    def half(i, f):
        start = pl.multiple_of(place(i, f) * width, width)
        block = jnp.dot(a_ref[...].reshape(own * rows, cols), r_ref[:, pl.ds(start, width)],
                        preferred_element_type=jnp.float32)
        return block.astype(jnp.bfloat16).reshape(own, npair, strip, width)

    def rotate(s, carry):
        i, f = s // CORES, s % CORES
        h_ref[s] = half(i, f)
        for e in peers[::-1] + (0,):
            swap_copy(s, i, f, e).start()
        return carry

    def in_rows(s, position):
        return g_ref.at[s, :, position, pl.ds(early, late), :]

    def in_copy(s, e):
        return remote(in_rows(s, partner(e)), x_ref.at[s, pair], in_send.at[0], in_recv.at[s], partner(e), mat)

    def in_local(s):
        return pltpu.make_async_copy(in_rows(s, pair), x_ref.at[s, pair], in_recv.at[s])

    def out_rows(s, start, count):
        at = flip(core, s % CORES, CORES) * rows + pair * strip + start
        return z_ref.at[s // CORES, :, pl.ds(pl.multiple_of(at, BLOCK), count), :]

    def pass_copy(s, e):
        return remote(g_ref.at[s, :, partner(e), pl.ds(0, early), :], out_rows(s, 0, early),
                      pass_send.at[0], out_recv.at[s], partner(e), mat)

    def pass_local(s):
        return pltpu.make_async_copy(g_ref.at[s, :, pair, pl.ds(0, early), :], out_rows(s, 0, early),
                                     out_recv.at[s])

    def out_copy(s, e):
        return remote(y_ref.at[s, partner(e)], out_rows(s, early, late), out_send.at[0], out_recv.at[s],
                      partner(e), mat)

    def out_local(s):
        return pltpu.make_async_copy(y_ref.at[s, pair], out_rows(s, early, late), out_recv.at[s])

    def enter(s):
        for e in peers[::-1] + (0,):
            if s > 0:
                swap_copy(s, s // CORES, s % CORES, e).wait_recv()
            if e:
                launch(lambda e=e: in_copy(s, e))
        in_local(s).start()
        if early:
            for e in peers[::-1]:
                launch(lambda e=e: pass_copy(s, e))
            pass_local(s).start()

    def mix(s):
        await_bytes(x_ref.at[s], in_recv.at[s])

        def chunk(b, carry):
            at = pl.ds(pl.multiple_of(b * BLOCK, BLOCK), BLOCK)
            block = x_ref[s, :, :, at, :].reshape(nsel * BLOCK, width)
            mixed = jnp.dot(kron_ref[...], block, preferred_element_type=jnp.float32)
            y_ref[s, :, :, at, :] = mixed.astype(jnp.bfloat16).reshape(npair, ntg, BLOCK, width)
            return carry

        lax.fori_loop(0, late // BLOCK, chunk, 0)
        for e in peers[::-1]:
            launch(lambda e=e: out_copy(s, e))
        out_local(s).start()

    tile = cols

    def arrived(s):
        await_bytes(z_ref.at[s // CORES, :, pl.ds(0, rows), :], out_recv.at[s])

    steps = cols // tile

    def product(i, f, add, last):
        source = flip(line, offset_of(i, nline), nline)
        if f is None:
            depth = pl.ds(0, CORES * rows)
        else:
            depth = pl.ds(pl.multiple_of(flip(core, f, CORES) * rows, rows), rows)

        def target(n, carry):
            t, at = n // steps, pl.ds(pl.multiple_of(n % steps * tile, tile), tile)
            part = jnp.dot(lt_ref[source, at, depth], z_ref[i, t, depth, :], preferred_element_type=jnp.float32)
            if add:
                part = part + acc_ref[t, at, :]
            if last:
                stage_ref[t, at, :] = part.astype(jnp.bfloat16)
            else:
                acc_ref[t, at, :] = part
            return carry

        return target

    def finish(i):
        for f in range(CORES):
            arrived(i * CORES + f)
        lax.fori_loop(0, ntg * steps, product(i, None, i > 0, False), 0)

    def finish_last():
        i = nline - 1
        for f in range(CORES):
            arrived(i * CORES + f)
            if f < CORES - 1:
                lax.fori_loop(0, ntg * steps, product(i, f, i + f > 0, False), 0)
        for t in range(ntg):
            lax.fori_loop(t * steps, (t + 1) * steps, product(i, CORES - 1, True, True), 0)

    lax.fori_loop(CORES, 2 * CORES, rotate, 0)
    for h in range(2, nline - 1):
        left_hop(h)
    for h in hops:
        spread_second(near, h)
    for h in range(1, nline - 1):
        left_first(h)
    for h in hops:
        spread_third(near, h)
    spread_last(near)
    g_ref[0] = half(0, 0)
    enter(0)
    lax.fori_loop(1, CORES, rotate, 0)
    enter(1)
    lax.fori_loop(2 * CORES, min(3 * CORES, nmat), rotate, 0)
    for e in peers:
        launch(lambda e=e: next_copy(e))
    lax.fori_loop(min(3 * CORES, nmat), nmat, rotate, 0)

    for i in range(nline):
        first = i * CORES
        if i > 0:
            for f in range(CORES):
                enter(first + f)
        if i == min(3, nline - 1):
            left_beside()
        for f in range(CORES):
            mix(first + f)
            stage = i * CORES + f
            last = nline - 1
            if stage == 0:
                for h in range(1, last):
                    spread_second(LEFT, h)
                left_first(last)
            if stage == 1:
                for h in range(1, last):
                    spread_third(LEFT, h)
            if stage == 2:
                spread_second(LEFT, last)
            if stage == min(4, nmat - 1):
                spread_third(LEFT, last)
            if i > 0 and f == (CORES - 1 if i == nline - 1 else 0):
                if i == 1:
                    core_whole(LEFT).wait_recv()
                if i == min(2, nline - 1):
                    spread_last(LEFT)
                if i == min(3, nline - 1):
                    spread_last(BESIDE)
                finish(i - 1)
    finish_last()

    count = (nline - 1) * (npair - 1)
    for m in range(2):
        await_bytes(r_ref.at[pl.ds(0, count * strip), pl.ds(0, cols // 2)], plane_send.at[m])
    if nline > 2:
        await_bytes(lt_ref.at[pl.ds(0, nline - 2), pl.ds(0, (npair - 1) * mpiece), pl.ds(0, rows)],
                    plane_send.at[LEFT])
        await_bytes(gathered(LEFT), core_send.at[LEFT])
    await_bytes(lt_ref.at[0, pl.ds(0, (npair - 1) * mpiece), pl.ds(0, rows)], next_send.at[0])
    for m in (0, 1, BESIDE):
        await_bytes(gathered(m), core_send.at[m])
    for m in (0, LEFT):
        core_whole(m).wait_send()
    await_bytes(h_ref.at[pl.ds(1, nmat - 1)], swap_send.at[0])
    await_bytes(x_ref.at[:, pl.ds(0, npair - 1)], in_send.at[0])
    await_bytes(y_ref.at[:, pl.ds(0, npair - 1)], out_send.at[0])
    if early:
        await_bytes(early_ref.at[pl.ds(0, npair - 1)], first_send.at[0])
        await_bytes(g_ref.at[:, :, pl.ds(0, npair - 1), pl.ds(0, early), :], pass_send.at[0])
    for make, cond in chained:
        pl.when(cond)(lambda make=make: make().wait_send())


def shards(operators, left_rot, right_rot, integrals, pair_index, target_index):
    npair, nmat = lax.axis_size("pair"), lax.axis_size("mat")
    nline = nmat // CORES
    own, rows, cols = operators.shape
    width = cols // nmat
    strip = rows // npair
    early = early_rows(own, target_index.shape[0] // npair, strip)
    ntgt, nsel = target_index.shape[0], pair_index.shape[0]
    ntg = ntgt // npair
    bf16, f32 = jnp.bfloat16, jnp.float32
    dma = pltpu.SemaphoreType.DMA
    anywhere = pl.BlockSpec(memory_space=pl.ANY)
    scalars = pl.BlockSpec(memory_space=pltpu.SMEM)
    return pl.pallas_call(
        functools.partial(kernel, npair, nline),
        out_shape=pltpu.VMEM((ntg, cols, width), bf16),
        in_specs=[scalars, scalars, anywhere, anywhere, anywhere, anywhere],
        out_specs=pl.BlockSpec(memory_space=pltpu.VMEM),
        scratch_shapes=[
            pltpu.VMEM((own, npair, strip, cols), bf16),
            pltpu.VMEM((npair, own, BLOCK, cols), bf16),
            pltpu.VMEM((cols, cols), bf16),
            pltpu.VMEM((rows, cols), bf16),
            pltpu.VMEM((nline, cols, CORES * rows), bf16),
            pltpu.VMEM(integrals.shape, f32),
            pltpu.VMEM((ntgt, integrals.shape[1]), f32),
            pltpu.VMEM((ntgt * BLOCK, nsel * BLOCK), bf16),
            pltpu.VMEM((nmat, own, npair, strip, width), bf16),
            pltpu.VMEM((nmat, own, npair, strip, width), bf16),
            pltpu.VMEM((nmat, npair, own, strip - early, width), bf16),
            pltpu.VMEM((nmat, npair, ntg, strip - early, width), bf16),
            pltpu.VMEM((nline, ntg, CORES * rows, width), bf16),
            pltpu.VMEM((ntg, cols, width), f32),
            dma((4,)),
            dma((3, nline, 2)), dma((3, nline)),
            dma((3,)), dma((3, nline, npair)),
            dma((4,)), dma((4,)), dma((2,)), dma((2,)),
            dma((1,)), dma((1,)),
            dma((1,)), dma((nmat, npair)),
            dma((1,)), dma((1,)),
            dma((1,)), dma((nmat,)),
            dma((1,)), dma((1,)), dma((nmat,)),
        ],
        compiler_params=pltpu.CompilerParams(
            collective_id=0, has_side_effects=True, vmem_limit_bytes=56623104),
    )(target_index, pair_index, operators.reshape(own, npair, strip, cols), right_rot, left_rot, integrals)


def solution(mesh):
    in_specs = (P("pair", "mat", None), P("mat", None), P("mat", None), P(), P(), P())
    out_specs = P("pair", None, "mat")
    return jax.shard_map(shards, mesh=mesh, in_specs=in_specs, out_specs=out_specs, check_vma=False)
```

```python
import functools

import jax
import jax.numpy as jnp
from jax import lax
from jax.experimental import pallas as pl
from jax.experimental.pallas import tpu as pltpu
from jax.sharding import PartitionSpec as P

CORES = 2
NEAR = 2
BLOCK = 16
BESIDE = 3
LEFT = 2
UP, DOWN = 0, 1
MESH_ID = pl.DeviceIdType.MESH


def flip(index, offset, count):
    total, bit = 0, 1
    while bit < count:
        total = total + bit * ((index // bit + offset // bit) % 2)
        bit *= 2
    return total


def offset_of(i, line, nline):
    if nline == 4 and i % 2 == 1:
        inner = (line + 1) // 2 % 2
        return 3 - inner if i == 1 else 2 + inner
    return 0 if i == 0 else (nline - 1 - (i - 1) // 2 if i % 2 == 1 else i // 2)


def order_of(d, line, nline):
    if nline == 4 and d >= 2:
        return 1 + 2 * ((line + 1) // 2 % 2)
    return next(i for i in range(nline) if offset_of(i, 0, nline) == d)


def early_rows(own, ntg, strip):
    return BLOCK if own == ntg and strip > BLOCK else 0


def kernel(npair, nline, targets_ref, pairs_ref, a_hbm, r_hbm, l_hbm, integrals_hbm, stage_ref,
           a_ref, early_ref, r_ref, l_ref, lt_ref, integrals_ref, rows_ref, kron_ref, h_ref, g_ref, x_ref, y_ref, z_ref,
           acc_ref,
           load_sem, line_send, line_recv, plane_send, plane_recv, core_send, core_recv, whole_send, whole_recv,
           next_send, next_recv,
           swap_send, swap_recv, first_send, first_recv, in_send, in_recv, pass_send, out_send, out_recv):
    own, _, strip, cols = a_hbm.shape
    rows = npair * strip
    ntgt, nsel = targets_ref.shape[0], pairs_ref.shape[0]
    ntg = ntgt // npair
    nmat = nline * CORES
    width = cols // nmat
    early = early_rows(own, ntg, strip)
    late = strip - early
    mpiece = cols // npair
    pair, mat = lax.axis_index("pair"), lax.axis_index("mat")
    line, core = mat // CORES, mat % CORES
    peers = tuple(range(1, npair))
    straight = tuple(e for e in peers if e % NEAR == 0 or e // NEAR == 0)
    far = tuple(e for e in peers if e not in straight)
    hops = range(1, nline)

    def place(i, f):
        return flip(line, offset_of(i, line, nline), nline) * CORES + flip(core, f, CORES)

    def partner(e):
        return flip(pair, e, npair)

    sibling = line * CORES + flip(core, 1, CORES)

    def remote(src, dst, send, recv, pair_id, mat_id):
        return pltpu.make_async_remote_copy(
            src_ref=src, dst_ref=dst, send_sem=send, recv_sem=recv,
            device_id={"pair": pair_id, "mat": mat_id}, device_id_type=MESH_ID)

    def launch(make, cond=None):
        if cond is None:
            make().start()
        else:
            pl.when(cond)(lambda: make().start())

    def await_bytes(block, sem):
        pltpu.make_async_copy(block, block, sem).wait()

    chained = []

    load_r = pltpu.make_async_copy(r_hbm, r_ref.at[pl.ds(pl.multiple_of(mat * rows, rows), rows), :], load_sem.at[0])
    load_l = pltpu.make_async_copy(l_hbm, l_ref, load_sem.at[1])
    load_i = pltpu.make_async_copy(integrals_hbm, integrals_ref, load_sem.at[2])
    load_a = pltpu.make_async_copy(a_hbm, a_ref, load_sem.at[3])
    for copy in (load_l, load_i, load_r, load_a):
        copy.start()

    barrier = pltpu.get_barrier_semaphore()

    def greet(pair_id, mat_id):
        pl.semaphore_signal(barrier, inc=1, device_id={"pair": pair_id, "mat": mat_id}, device_id_type=MESH_ID)

    for e in peers:
        greet(partner(e), mat)
    greet(pair, sibling)
    pl.when(line > 0)(lambda: greet(pair, mat - CORES))
    pl.when(line < nline - 1)(lambda: greet(pair, mat + CORES))
    above, below = 1 - (line + 1) // nline, (line + nline - 1) // nline
    pl.semaphore_wait(barrier, len(peers) + 1 + above + below)

    def piece(m, source, c, origin, part=None):
        if m is not LEFT:
            at = pl.multiple_of((source * CORES + c) * rows + origin * strip, strip)
            size = cols // 2 if part is None else cols // 4
            start = m * (cols // 2) + (0 if part is None else part * size)
            return r_ref.at[pl.ds(at, strip), pl.ds(pl.multiple_of(start, size), size)]
        lanes = pl.ds(pl.multiple_of(c * rows, rows), rows)
        at = pl.multiple_of(origin * mpiece, mpiece)
        if part is None:
            return lt_ref.at[source, pl.ds(at, mpiece), lanes]
        at = pl.multiple_of(at + part * (mpiece // 2), mpiece // 2)
        return lt_ref.at[source, pl.ds(at, mpiece // 2), lanes]

    def own_piece(m):
        if m is not LEFT:
            return r_hbm.at[pl.ds(pl.multiple_of(pair * strip, strip), strip), pl.ds(m * (cols // 2), cols // 2)]
        return piece(LEFT, line, core, pair)

    def chain_copy(m, source, way, first):
        block = piece(m, source, core, pair)
        step = 1 if way == UP else -1
        return remote(own_piece(m) if first else block, block, line_send.at[m, source, way], line_recv.at[m, source],
                      pair, (line + step) * CORES + core)

    def line_arrival(m, source):
        block = piece(m, source, core, pair)
        return remote(block, block, line_send.at[m, source, UP], line_recv.at[m, source], pair, sibling)

    def plane_copy(m, source, to, origin, part=None):
        block = piece(m, source, core, partner(origin), part)
        k = to ^ origin
        return remote(block, block, plane_send.at[m], plane_recv.at[m, source, k], partner(to), mat)

    def plane_arrival(m, source, e):
        block = piece(m, source, core, partner(e))
        return remote(block, block, plane_send.at[m], plane_recv.at[m, source, e], partner(e), mat)

    def core_copy(m, source, e, group=None):
        block = piece(m, source, core, partner(e))
        k = m if group is None else group
        return remote(block, block, core_send.at[k], core_recv.at[k], pair, sibling)

    def core_whole(m):
        if m is not LEFT:
            src, dst = r_hbm, r_ref.at[pl.ds(pl.multiple_of(mat * rows, rows), rows), :]
        else:
            src = dst = lt_ref.at[line, :, pl.ds(pl.multiple_of(core * rows, rows), rows)]
        k = 1 if m is LEFT else 0
        return remote(src, dst, whole_send.at[k], whole_recv.at[k], pair, sibling)

    def reaches(way, h):
        if way == UP:
            return line >= h, line - h
        return line + h < nline, line + h

    def both(h, act):
        for way in (UP, DOWN):
            cond, source = reaches(way, h)
            act(way, cond, source)

    def chain(make, cond):
        chained.append((make, cond))
        launch(make, cond)

    def hop(m, h, ways=(UP, DOWN)):
        for way in ways:
            cond, source = reaches(way, h)
            pl.when(cond)(lambda: line_arrival(m, source).wait_recv())
            if h + 1 < nline:
                more = line < nline - 1 if way == UP else line > 0
                chain(lambda m=m, source=source, way=way: chain_copy(m, source, way, False), cond & more)

    def left_hop(h):
        if h + 1 < nline:
            for way in (UP, DOWN):
                cond, source = reaches(way, h)
                more = cond & (line < nline - 1 if way == UP else line > 0)
                pl.when(more)(lambda: line_arrival(LEFT, source).wait_recv())
                chain(lambda source=source, way=way: chain_copy(LEFT, source, way, False), more)

    def spread_way(m, way, cond, source):
        for e in straight:
            launch(lambda e=e: plane_copy(m, source, e, 0), cond)
        launch(lambda: core_copy(m, source, 0), cond)

    def spread_first(m, h):
        both(h, lambda way, cond, source: spread_way(m, way, cond, source))

    beside = flip(line, 1, nline)

    def next_copy(e):
        block = piece(LEFT, line, core, partner(e))
        return remote(block, block, next_send.at[0], next_recv.at[0], pair, beside * CORES + core)

    def left_first(h):
        def act(way, cond, source):
            ends = cond if h + 1 == nline else cond & (line == (nline - 1 if way == UP else 0))
            pl.when(ends)(lambda: line_arrival(LEFT, source).wait_recv())
            if h == 1:
                through = cond & (line % 2 == (0 if way == UP else 1))
                launch(lambda: core_copy(LEFT, source, 0, BESIDE), cond & (line % 2 == (1 if way == UP else 0)))
            else:
                through = cond
            spread_way(LEFT, way, through, source)
        both(h, act)

    def left_beside():
        await_bytes(lt_ref.at[0, pl.ds(0, (npair - 1) * mpiece), pl.ds(0, rows)], next_recv.at[0])
        for e in peers:
            launch(lambda e=e: core_copy(LEFT, beside, e, BESIDE))

    def spread_second(m, h):
        def act(way, cond, source):
            if m is LEFT and h == 1:
                cond = cond & (line % 2 == (0 if way == UP else 1))
            for e in straight:
                pl.when(cond)(lambda e=e: plane_arrival(m, source, e).wait_recv())
                for to in straight:
                    if to ^ e in far:
                        launch(lambda e=e, to=to: plane_copy(m, source, to, e, 0 if e < NEAR else 1), cond)
                launch(lambda e=e: core_copy(m, source, e), cond)
        both(h, act)

    def spread_third(m, h):
        def act(way, cond, source):
            if m is LEFT and h == 1:
                cond = cond & (line % 2 == (0 if way == UP else 1))
            for e in far:
                pl.when(cond)(lambda e=e: plane_arrival(m, source, e).wait_recv())
                launch(lambda e=e: core_copy(m, source, e), cond)
        both(h, act)

    def gathered(m):
        if m is BESIDE:
            return lt_ref.at[0, :, pl.ds(0, rows)]
        if m is LEFT:
            return lt_ref.at[pl.ds(0, nline - 2), :, pl.ds(0, rows)]
        return r_ref.at[pl.ds(0, (nline - 1) * rows), pl.ds(0, cols // 2)]

    def spread_last(m):
        if m is not LEFT or nline > 2:
            await_bytes(gathered(m), core_recv.at[m])

    def depart(m, way):
        chain(lambda: chain_copy(m, line, way, True), line < nline - 1 if way == UP else line > 0)

    def early_source(position):
        return a_hbm.at[:, position, pl.ds(0, early), :]

    def early_copy(e):
        return remote(early_source(partner(e)), early_ref.at[pair], first_send.at[0], first_recv.at[0],
                      partner(e), mat)

    def early_mix():
        await_bytes(early_ref, first_recv.at[0])
        load_a.wait()
        span = min(512, cols)

        def columns(b, carry):
            at = pl.ds(pl.multiple_of(b * span, span), span)
            mixed = jnp.dot(kron_ref[...], early_ref[:, :, :, at].reshape(nsel * BLOCK, span),
                            preferred_element_type=jnp.float32)
            mixed = mixed.astype(jnp.bfloat16).reshape(npair, ntg, BLOCK, span)
            for position in range(npair):
                a_ref[:, position, pl.ds(0, early), at] = mixed[position]
            return carry

        lax.fori_loop(0, cols // span, columns, 0)

    for turn_of in range(2):
        depart(turn_of, UP)
        depart(1 - turn_of, DOWN)
    launch(lambda: core_whole(0))
    if early:
        for e in peers[::-1]:
            launch(lambda e=e: early_copy(e))
        pltpu.make_async_copy(early_source(pair), early_ref.at[pair], first_recv.at[0]).start()

    load_l.wait()
    lanes = pl.ds(pl.multiple_of(core * rows, rows), rows)

    def turn(b, carry):
        at = pl.ds(pl.multiple_of(b * 256, 256), 256)
        lt_ref[line, at, lanes] = l_ref[:, at].T
        return carry

    lax.fori_loop(0, cols // 256, turn, 0)

    load_i.wait()
    for t in range(ntgt):
        rows_ref[pl.ds(t, 1), :] = integrals_ref[pl.ds(targets_ref[t], 1), :]
    picked = rows_ref[...]
    lane = lax.broadcasted_iota(jnp.int32, picked.shape, 1)
    column = lax.broadcasted_iota(jnp.int32, (ntgt, nsel), 1)
    coupling = jnp.zeros((ntgt, nsel), jnp.float32)
    for k in range(nsel):
        value = jnp.sum(jnp.where(lane == pairs_ref[k], picked, 0.0), axis=1, keepdims=True)
        coupling = jnp.where(column == k, value, coupling)
    down = lax.broadcasted_iota(jnp.int32, (ntgt * BLOCK, ntgt), 0) // BLOCK
    tall = (down == lax.broadcasted_iota(jnp.int32, (ntgt * BLOCK, ntgt), 1)).astype(jnp.bfloat16)
    across = lax.broadcasted_iota(jnp.int32, (nsel, nsel * BLOCK), 1) // BLOCK
    broad = (across == lax.broadcasted_iota(jnp.int32, (nsel, nsel * BLOCK), 0)).astype(jnp.bfloat16)
    wide = jnp.dot(coupling.astype(jnp.bfloat16), broad, preferred_element_type=jnp.float32).astype(jnp.bfloat16)
    full = jnp.dot(tall, wide, preferred_element_type=jnp.float32)
    same = (lax.broadcasted_iota(jnp.int32, full.shape, 0) % BLOCK
            == lax.broadcasted_iota(jnp.int32, full.shape, 1) % BLOCK)
    kron_ref[...] = jnp.where(same, full, 0.0).astype(jnp.bfloat16)

    near = line // (nline // 2)
    away = 1 - near

    def hop_right(h, turn_of):
        for way, m in ((UP, turn_of), (DOWN, 1 - turn_of)):
            hop(m, h, (way,))
            cond, source = reaches(way, h)
            spread_way(m, way, cond & (away == m), source)

    for h in range(1, nline - 1):
        hop_right(h, 0)
        hop_right(h, 1)
    depart(LEFT, UP)
    depart(LEFT, DOWN)
    launch(lambda: core_whole(LEFT))
    hop_right(nline - 1, 0)
    if early:
        early_mix()
    for h in range(1, nline - 1):
        spread_second(away, h)
    left_hop(1)
    spread_second(away, nline - 1)
    hop_right(nline - 1, 1)
    for h in hops:
        spread_first(near, h)
    for h in hops:
        spread_third(away, h)
    load_r.wait()
    if not early:
        load_a.wait()
    core_whole(0).wait_recv()
    spread_last(away)

    def swap_copy(d, f, e):
        strips = partner(e)
        slot = order_of(d, line, nline) * CORES + f
        there = flip(line, d, nline) * CORES + flip(core, f, CORES)
        return remote(h_ref.at[d * CORES + f, :, strips], g_ref.at[slot, :, strips], swap_send.at[0],
                      swap_recv.at[slot, e], pair, there)

    def swap_arrival(s, e):
        block = g_ref.at[s, :, partner(e)]
        return remote(block, block, swap_send.at[0], swap_recv.at[s, e], pair, sibling)

    def half(d, f):
        there = flip(line, d, nline) * CORES + flip(core, f, CORES)
        start = pl.multiple_of(there * width, width)
        block = jnp.dot(a_ref[...].reshape(own * rows, cols), r_ref[:, pl.ds(start, width)],
                        preferred_element_type=jnp.float32)
        return block.astype(jnp.bfloat16).reshape(own, npair, strip, width)

    def rotate(d, first=0):
        def one(f, carry):
            h_ref[d * CORES + f] = half(d, f)
            for e in peers[::-1] + (0,):
                swap_copy(d, f, e).start()
            return carry

        lax.fori_loop(first, CORES, one, 0)

    def in_rows(s, position):
        return g_ref.at[s, :, position, pl.ds(early, late), :]

    def in_copy(s, e):
        return remote(in_rows(s, partner(e)), x_ref.at[s, pair], in_send.at[0], in_recv.at[s], partner(e), mat)

    def in_local(s):
        return pltpu.make_async_copy(in_rows(s, pair), x_ref.at[s, pair], in_recv.at[s])

    def out_rows(s, start, count):
        at = flip(core, s % CORES, CORES) * rows + pair * strip + start
        return z_ref.at[s // CORES, :, pl.ds(pl.multiple_of(at, BLOCK), count), :]

    def pass_copy(s, e):
        return remote(g_ref.at[s, :, partner(e), pl.ds(0, early), :], out_rows(s, 0, early),
                      pass_send.at[0], out_recv.at[s], partner(e), mat)

    def pass_local(s):
        return pltpu.make_async_copy(g_ref.at[s, :, pair, pl.ds(0, early), :], out_rows(s, 0, early),
                                     out_recv.at[s])

    def out_copy(s, e):
        return remote(y_ref.at[s, partner(e)], out_rows(s, early, late), out_send.at[0], out_recv.at[s],
                      partner(e), mat)

    def out_local(s):
        return pltpu.make_async_copy(y_ref.at[s, pair], out_rows(s, early, late), out_recv.at[s])

    def enter(s):
        for e in peers[::-1] + (0,):
            if s > 0:
                swap_arrival(s, e).wait_recv()
            if e:
                launch(lambda e=e: in_copy(s, e))
        in_local(s).start()
        if early:
            for e in peers[::-1]:
                launch(lambda e=e: pass_copy(s, e))
            pass_local(s).start()

    def mix(s):
        await_bytes(x_ref.at[s], in_recv.at[s])

        def chunk(b, carry):
            at = pl.ds(pl.multiple_of(b * BLOCK, BLOCK), BLOCK)
            block = x_ref[s, :, :, at, :].reshape(nsel * BLOCK, width)
            mixed = jnp.dot(kron_ref[...], block, preferred_element_type=jnp.float32)
            y_ref[s, :, :, at, :] = mixed.astype(jnp.bfloat16).reshape(npair, ntg, BLOCK, width)
            return carry

        lax.fori_loop(0, late // BLOCK, chunk, 0)
        for e in peers[::-1]:
            launch(lambda e=e: out_copy(s, e))
        out_local(s).start()

    tile = cols

    def arrived(s):
        await_bytes(z_ref.at[s // CORES, :, pl.ds(0, rows), :], out_recv.at[s])

    steps = cols // tile

    def product(i, f, add, last):
        source = flip(line, offset_of(i, line, nline), nline)
        if f is None:
            depth = pl.ds(0, CORES * rows)
        else:
            depth = pl.ds(pl.multiple_of(flip(core, f, CORES) * rows, rows), rows)

        def target(n, carry):
            t, at = n // steps, pl.ds(pl.multiple_of(n % steps * tile, tile), tile)
            part = jnp.dot(lt_ref[source, at, depth], z_ref[i, t, depth, :], preferred_element_type=jnp.float32)
            if add:
                part = part + acc_ref[t, at, :]
            if last:
                stage_ref[t, at, :] = part.astype(jnp.bfloat16)
            else:
                acc_ref[t, at, :] = part
            return carry

        return target

    def finish(i):
        for f in range(CORES):
            arrived(i * CORES + f)
        lax.fori_loop(0, ntg * steps, product(i, None, i > 0, False), 0)

    def finish_last():
        i = nline - 1
        for f in range(CORES):
            arrived(i * CORES + f)
            if f < CORES - 1:
                lax.fori_loop(0, ntg * steps, product(i, f, i + f > 0, False), 0)
        for t in range(ntg):
            lax.fori_loop(t * steps, (t + 1) * steps, product(i, CORES - 1, True, True), 0)

    for d in range(nline - 1, nline // 2 - 1, -1):
        rotate(d)
    for h in range(2, nline - 1):
        left_hop(h)
    for h in hops:
        spread_second(near, h)
    for h in range(1, nline - 1):
        left_first(h)
    for h in hops:
        spread_third(near, h)
    spread_last(near)
    g_ref[0] = half(0, 0)
    enter(0)
    rotate(0, 1)
    enter(1)
    for d in range(1, nline // 2):
        rotate(d)
    for e in peers:
        launch(lambda e=e: next_copy(e))

    for i in range(nline):
        first = i * CORES
        if i > 0:
            for f in range(CORES):
                enter(first + f)
        if i == min(3, nline - 1):
            left_beside()
        for f in range(CORES):
            mix(first + f)
            stage = i * CORES + f
            last = nline - 1
            if stage == 0:
                for h in range(1, last):
                    spread_second(LEFT, h)
                left_first(last)
            if stage == 1:
                for h in range(1, last):
                    spread_third(LEFT, h)
            if stage == 2:
                spread_second(LEFT, last)
            if stage == min(4, nmat - 1):
                spread_third(LEFT, last)
            if i > 0 and f == (CORES - 1 if i == nline - 1 else 0):
                if i == 1:
                    core_whole(LEFT).wait_recv()
                if i == min(2, nline - 1):
                    spread_last(LEFT)
                if i == min(3, nline - 1):
                    spread_last(BESIDE)
                finish(i - 1)
    finish_last()

    count = (nline - 1) * (npair - 1)
    for m in range(2):
        await_bytes(r_ref.at[pl.ds(0, count * strip), pl.ds(0, cols // 2)], plane_send.at[m])
    if nline > 2:
        await_bytes(lt_ref.at[pl.ds(0, nline - 2), pl.ds(0, (npair - 1) * mpiece), pl.ds(0, rows)],
                    plane_send.at[LEFT])
        await_bytes(gathered(LEFT), core_send.at[LEFT])
    await_bytes(lt_ref.at[0, pl.ds(0, (npair - 1) * mpiece), pl.ds(0, rows)], next_send.at[0])
    for m in (0, 1, BESIDE):
        await_bytes(gathered(m), core_send.at[m])
    for m in (0, LEFT):
        core_whole(m).wait_send()
    await_bytes(h_ref.at[pl.ds(1, nmat - 1)], swap_send.at[0])
    await_bytes(x_ref.at[:, pl.ds(0, npair - 1)], in_send.at[0])
    await_bytes(y_ref.at[:, pl.ds(0, npair - 1)], out_send.at[0])
    if early:
        await_bytes(early_ref.at[pl.ds(0, npair - 1)], first_send.at[0])
        await_bytes(g_ref.at[:, :, pl.ds(0, npair - 1), pl.ds(0, early), :], pass_send.at[0])
    for make, cond in chained:
        pl.when(cond)(lambda make=make: make().wait_send())


def shards(operators, left_rot, right_rot, integrals, pair_index, target_index):
    npair, nmat = lax.axis_size("pair"), lax.axis_size("mat")
    nline = nmat // CORES
    own, rows, cols = operators.shape
    width = cols // nmat
    strip = rows // npair
    early = early_rows(own, target_index.shape[0] // npair, strip)
    ntgt, nsel = target_index.shape[0], pair_index.shape[0]
    ntg = ntgt // npair
    bf16, f32 = jnp.bfloat16, jnp.float32
    dma = pltpu.SemaphoreType.DMA
    anywhere = pl.BlockSpec(memory_space=pl.ANY)
    scalars = pl.BlockSpec(memory_space=pltpu.SMEM)
    return pl.pallas_call(
        functools.partial(kernel, npair, nline),
        out_shape=pltpu.VMEM((ntg, cols, width), bf16),
        in_specs=[scalars, scalars, anywhere, anywhere, anywhere, anywhere],
        out_specs=pl.BlockSpec(memory_space=pltpu.VMEM),
        scratch_shapes=[
            pltpu.VMEM((own, npair, strip, cols), bf16),
            pltpu.VMEM((npair, own, BLOCK, cols), bf16),
            pltpu.VMEM((cols, cols), bf16),
            pltpu.VMEM((rows, cols), bf16),
            pltpu.VMEM((nline, cols, CORES * rows), bf16),
            pltpu.VMEM(integrals.shape, f32),
            pltpu.VMEM((ntgt, integrals.shape[1]), f32),
            pltpu.VMEM((ntgt * BLOCK, nsel * BLOCK), bf16),
            pltpu.VMEM((nmat, own, npair, strip, width), bf16),
            pltpu.VMEM((nmat, own, npair, strip, width), bf16),
            pltpu.VMEM((nmat, npair, own, strip - early, width), bf16),
            pltpu.VMEM((nmat, npair, ntg, strip - early, width), bf16),
            pltpu.VMEM((nline, ntg, CORES * rows, width), bf16),
            pltpu.VMEM((ntg, cols, width), f32),
            dma((4,)),
            dma((3, nline, 2)), dma((3, nline)),
            dma((3,)), dma((3, nline, npair)),
            dma((4,)), dma((4,)), dma((2,)), dma((2,)),
            dma((1,)), dma((1,)),
            dma((1,)), dma((nmat, npair)),
            dma((1,)), dma((1,)),
            dma((1,)), dma((nmat,)),
            dma((1,)), dma((1,)), dma((nmat,)),
        ],
        compiler_params=pltpu.CompilerParams(
            collective_id=0, has_side_effects=True, vmem_limit_bytes=56623104),
    )(target_index, pair_index, operators.reshape(own, npair, strip, cols), right_rot, left_rot, integrals)


def solution(mesh):
    in_specs = (P("pair", "mat", None), P("mat", None), P("mat", None), P(), P(), P())
    out_specs = P("pair", None, "mat")
    return jax.shard_map(shards, mesh=mesh, in_specs=in_specs, out_specs=out_specs, check_vma=False)
```

```python
import functools

import jax
import jax.numpy as jnp
from jax import lax
from jax.experimental import pallas as pl
from jax.experimental.pallas import tpu as pltpu
from jax.sharding import PartitionSpec as P

CORES = 2
NEAR = 2
BLOCK = 16
BESIDE = 3
LEFT = 2
UP, DOWN = 0, 1
MESH_ID = pl.DeviceIdType.MESH


def flip(index, offset, count):
    total, bit = 0, 1
    while bit < count:
        total = total + bit * ((index // bit + offset // bit) % 2)
        bit *= 2
    return total


def offset_of(i, line, nline):
    if nline == 4 and i % 2 == 1:
        inner = (line + 1) // 2 % 2
        return 3 - inner if i == 1 else 2 + inner
    return 0 if i == 0 else (nline - 1 - (i - 1) // 2 if i % 2 == 1 else i // 2)


def order_of(d, line, nline):
    if nline == 4 and d >= 2:
        return 1 + 2 * ((line + 1) // 2 % 2)
    return next(i for i in range(nline) if offset_of(i, 0, nline) == d)


def early_rows(own, ntg, strip):
    return BLOCK if own == ntg and strip > BLOCK else 0


def kernel(npair, nline, targets_hbm, pairs_hbm, a_hbm, r_hbm, l_hbm, integrals_hbm, stage_ref,
           targets_ref, pairs_ref, a_ref, early_ref, r_ref, l_ref, lt_ref, integrals_ref, rows_ref, kron_ref, h_ref, g_ref, x_ref, y_ref, z_ref,
           acc_ref,
           load_sem, line_send, line_recv, plane_send, plane_recv, core_send, core_recv, whole_send, whole_recv,
           next_send, next_recv,
           swap_send, swap_recv, first_send, first_recv, in_send, in_recv, pass_send, out_send, out_recv):
    own, _, strip, cols = a_hbm.shape
    rows = npair * strip
    ntgt, nsel = targets_hbm.shape[0], pairs_hbm.shape[0]
    ntg = ntgt // npair
    nmat = nline * CORES
    width = cols // nmat
    early = early_rows(own, ntg, strip)
    late = strip - early
    mpiece = cols // npair
    pair, mat = lax.axis_index("pair"), lax.axis_index("mat")
    line, core = mat // CORES, mat % CORES
    peers = tuple(range(1, npair))
    straight = tuple(e for e in peers if e % NEAR == 0 or e // NEAR == 0)
    far = tuple(e for e in peers if e not in straight)
    hops = range(1, nline)

    def place(i, f):
        return flip(line, offset_of(i, line, nline), nline) * CORES + flip(core, f, CORES)

    def partner(e):
        return flip(pair, e, npair)

    sibling = line * CORES + flip(core, 1, CORES)
    at_end = (line == 0) | (line == nline - 1)

    def remote(src, dst, send, recv, pair_id, mat_id):
        return pltpu.make_async_remote_copy(
            src_ref=src, dst_ref=dst, send_sem=send, recv_sem=recv,
            device_id={"pair": pair_id, "mat": mat_id}, device_id_type=MESH_ID)

    def launch(make, cond=None):
        if cond is None:
            make().start()
        else:
            pl.when(cond)(lambda: make().start())

    def await_bytes(block, sem):
        pltpu.make_async_copy(block, block, sem).wait()


    load_r = pltpu.make_async_copy(r_hbm, r_ref.at[pl.ds(pl.multiple_of(mat * rows, rows), rows), :], load_sem.at[0])
    load_l = pltpu.make_async_copy(l_hbm, l_ref, load_sem.at[1])
    load_i = pltpu.make_async_copy(integrals_hbm, integrals_ref, load_sem.at[2])
    load_a = pltpu.make_async_copy(a_hbm, a_ref, load_sem.at[3])
    load_t = pltpu.make_async_copy(targets_hbm, targets_ref, load_sem.at[4])
    load_p = pltpu.make_async_copy(pairs_hbm, pairs_ref, load_sem.at[5])
    for copy in (load_t, load_p, load_l, load_i, load_r, load_a):
        copy.start()

    barrier = pltpu.get_barrier_semaphore()

    def greet(pair_id, mat_id):
        pl.semaphore_signal(barrier, inc=1, device_id={"pair": pair_id, "mat": mat_id}, device_id_type=MESH_ID)

    for e in peers:
        greet(partner(e), mat)
    greet(pair, sibling)
    pl.when(line > 0)(lambda: greet(pair, mat - CORES))
    pl.when(line < nline - 1)(lambda: greet(pair, mat + CORES))
    above, below = 1 - (line + 1) // nline, (line + nline - 1) // nline
    pl.semaphore_wait(barrier, len(peers) + 1 + above + below)

    def piece(m, source, c, origin, part=None):
        if m is not LEFT:
            at = pl.multiple_of((source * CORES + c) * rows + origin * strip, strip)
            size = cols // 2 if part is None else cols // 4
            start = m * (cols // 2) + (0 if part is None else part * size)
            return r_ref.at[pl.ds(at, strip), pl.ds(pl.multiple_of(start, size), size)]
        lanes = pl.ds(pl.multiple_of(c * rows, rows), rows)
        at = pl.multiple_of(origin * mpiece, mpiece)
        if part is None:
            return lt_ref.at[source, pl.ds(at, mpiece), lanes]
        at = pl.multiple_of(at + part * (mpiece // 2), mpiece // 2)
        return lt_ref.at[source, pl.ds(at, mpiece // 2), lanes]

    def own_piece(m):
        if m is not LEFT:
            return r_hbm.at[pl.ds(pl.multiple_of(pair * strip, strip), strip), pl.ds(m * (cols // 2), cols // 2)]
        return piece(LEFT, line, core, pair)

    def chain_copy(m, source, way, first):
        block = piece(m, source, core, pair)
        step = 1 if way == UP else -1
        return remote(own_piece(m) if first else block, block, line_send.at[m], line_recv.at[m, source],
                      pair, (line + step) * CORES + core)

    def line_arrival(m, source):
        block = piece(m, source, core, pair)
        return remote(block, block, line_send.at[m], line_recv.at[m, source], pair, sibling)

    def plane_copy(m, source, to, origin, part=None):
        block = piece(m, source, core, partner(origin), part)
        k = to ^ origin
        return remote(block, block, plane_send.at[m], plane_recv.at[m, source, k - 1], partner(to), mat)

    def plane_arrival(m, source, e):
        block = piece(m, source, core, partner(e))
        return remote(block, block, plane_send.at[m], plane_recv.at[m, source, e - 1], partner(e), mat)

    def core_copy(m, source, e, group=None):
        block = piece(m, source, core, partner(e))
        k = m if group is None else group
        return remote(block, block, core_send.at[k], core_recv.at[k], pair, sibling)

    def core_whole(m):
        if m is not LEFT:
            src, dst = r_hbm, r_ref.at[pl.ds(pl.multiple_of(mat * rows, rows), rows), :]
        else:
            src = dst = lt_ref.at[line, :, pl.ds(pl.multiple_of(core * rows, rows), rows)]
        k = 1 if m is LEFT else 0
        return remote(src, dst, whole_send.at[k], whole_recv.at[k], pair, sibling)

    def reaches(way, h):
        if way == UP:
            return line >= h, line - h
        return line + h < nline, line + h

    def both(h, act):
        for way in (UP, DOWN):
            cond, source = reaches(way, h)
            act(way, cond, source)

    def hop(m, h, ways=(UP, DOWN)):
        for way in ways:
            cond, source = reaches(way, h)
            pl.when(cond)(lambda: line_arrival(m, source).wait_recv())
            if h + 1 < nline:
                more = line < nline - 1 if way == UP else line > 0
                launch(lambda m=m, source=source, way=way: chain_copy(m, source, way, False), cond & more)

    def left_hop(h):
        if h + 1 < nline:
            for way in (UP, DOWN):
                cond, source = reaches(way, h)
                more = cond & (line < nline - 1 if way == UP else line > 0)
                pl.when(more)(lambda: line_arrival(LEFT, source).wait_recv())
                launch(lambda source=source, way=way: chain_copy(LEFT, source, way, False), more)

    def spread_way(m, way, cond, source):
        for e in straight:
            launch(lambda e=e: plane_copy(m, source, e, 0), cond)
        launch(lambda: core_copy(m, source, 0), cond)

    def spread_first(m, h):
        both(h, lambda way, cond, source: spread_way(m, way, cond, source))

    beside = flip(line, 1, nline)

    def next_copy(e):
        block = piece(LEFT, line, core, partner(e))
        return remote(block, block, next_send.at[0], next_recv.at[0], pair, beside * CORES + core)

    def left_first(h):
        def act(way, cond, source):
            ends = cond if h + 1 == nline else cond & (line == (nline - 1 if way == UP else 0))
            pl.when(ends)(lambda: line_arrival(LEFT, source).wait_recv())
            if h == 1:
                through = cond & (line % 2 == (0 if way == UP else 1))
                launch(lambda: core_copy(LEFT, source, 0, BESIDE), cond & (line % 2 == (1 if way == UP else 0)))
            else:
                through = cond
            spread_way(LEFT, way, through, source)
        both(h, act)

    def left_beside():
        await_bytes(lt_ref.at[0, pl.ds(0, (npair - 1) * mpiece), pl.ds(0, rows)], next_recv.at[0])
        for e in peers:
            launch(lambda e=e: core_copy(LEFT, beside, e, BESIDE))

    def spread_second(m, h):
        def act(way, cond, source):
            if m is LEFT and h == 1:
                cond = cond & (line % 2 == (0 if way == UP else 1))
            for e in straight:
                pl.when(cond)(lambda e=e: plane_arrival(m, source, e).wait_recv())
                for to in straight:
                    if to ^ e in far:
                        launch(lambda e=e, to=to: plane_copy(m, source, to, e, 0 if e < NEAR else 1), cond)
                launch(lambda e=e: core_copy(m, source, e), cond)
        both(h, act)

    def spread_third(m, h):
        def act(way, cond, source):
            if m is LEFT and h == 1:
                cond = cond & (line % 2 == (0 if way == UP else 1))
            for e in far:
                pl.when(cond)(lambda e=e: plane_arrival(m, source, e).wait_recv())
                launch(lambda e=e: core_copy(m, source, e), cond)
        both(h, act)

    def gathered(m):
        if m is BESIDE:
            return lt_ref.at[0, :, pl.ds(0, rows)]
        if m is LEFT:
            return lt_ref.at[pl.ds(0, nline - 2), :, pl.ds(0, rows)]
        return r_ref.at[pl.ds(0, (nline - 1) * rows), pl.ds(0, cols // 2)]

    def spread_last(m):
        if m is not LEFT or nline > 2:
            await_bytes(gathered(m), core_recv.at[m])

    def depart(m, way):
        launch(lambda: chain_copy(m, line, way, True), line < nline - 1 if way == UP else line > 0)

    def early_source(position):
        return a_hbm.at[:, position, pl.ds(0, early), :]

    def early_copy(e):
        return remote(early_source(partner(e)), early_ref.at[pair], first_send.at[0], first_recv.at[0],
                      partner(e), mat)

    def early_mix():
        await_bytes(early_ref, first_recv.at[0])
        load_a.wait()
        span = min(512, cols)

        def columns(b, carry):
            at = pl.ds(pl.multiple_of(b * span, span), span)
            mixed = jnp.dot(kron_ref[...], early_ref[:, :, :, at].reshape(nsel * BLOCK, span),
                            preferred_element_type=jnp.float32)
            mixed = mixed.astype(jnp.bfloat16).reshape(npair, ntg, BLOCK, span)
            for position in range(npair):
                a_ref[:, position, pl.ds(0, early), at] = mixed[position]
            return carry

        lax.fori_loop(0, cols // span, columns, 0)

    for turn_of in range(2):
        depart(turn_of, UP)
        depart(1 - turn_of, DOWN)
    launch(lambda: core_whole(0))
    if early:
        for e in peers[::-1]:
            launch(lambda e=e: early_copy(e))
        pltpu.make_async_copy(early_source(pair), early_ref.at[pair], first_recv.at[0]).start()

    load_l.wait()
    lanes = pl.ds(pl.multiple_of(core * rows, rows), rows)

    def turn(b, carry):
        at = pl.ds(pl.multiple_of(b * 256, 256), 256)
        lt_ref[line, at, lanes] = l_ref[:, at].T
        return carry

    lax.fori_loop(0, cols // 256, turn, 0)

    load_i.wait()
    load_t.wait()
    load_p.wait()
    for t in range(ntgt):
        rows_ref[pl.ds(t, 1), :] = integrals_ref[pl.ds(targets_ref[t], 1), :]
    picked = rows_ref[...]
    lane = lax.broadcasted_iota(jnp.int32, picked.shape, 1)
    column = lax.broadcasted_iota(jnp.int32, (ntgt, nsel), 1)
    coupling = jnp.zeros((ntgt, nsel), jnp.float32)
    for k in range(nsel):
        value = jnp.sum(jnp.where(lane == pairs_ref[k], picked, 0.0), axis=1, keepdims=True)
        coupling = jnp.where(column == k, value, coupling)
    down = lax.broadcasted_iota(jnp.int32, (ntgt * BLOCK, ntgt), 0) // BLOCK
    tall = (down == lax.broadcasted_iota(jnp.int32, (ntgt * BLOCK, ntgt), 1)).astype(jnp.bfloat16)
    across = lax.broadcasted_iota(jnp.int32, (nsel, nsel * BLOCK), 1) // BLOCK
    broad = (across == lax.broadcasted_iota(jnp.int32, (nsel, nsel * BLOCK), 0)).astype(jnp.bfloat16)
    wide = jnp.dot(coupling.astype(jnp.bfloat16), broad, preferred_element_type=jnp.float32).astype(jnp.bfloat16)
    full = jnp.dot(tall, wide, preferred_element_type=jnp.float32)
    same = (lax.broadcasted_iota(jnp.int32, full.shape, 0) % BLOCK
            == lax.broadcasted_iota(jnp.int32, full.shape, 1) % BLOCK)
    kron_ref[...] = jnp.where(same, full, 0.0).astype(jnp.bfloat16)

    near = line // (nline // 2)
    away = 1 - near

    def hop_right(h, turn_of):
        for way, m in ((UP, turn_of), (DOWN, 1 - turn_of)):
            hop(m, h, (way,))
            cond, source = reaches(way, h)
            spread_way(m, way, cond & (away == m), source)

    for h in range(1, nline - 1):
        hop_right(h, 0)
        hop_right(h, 1)
    depart(LEFT, UP)
    depart(LEFT, DOWN)
    launch(lambda: core_whole(LEFT))
    hop_right(nline - 1, 0)
    if early:
        early_mix()
    for h in range(1, nline - 1):
        spread_second(away, h)
    left_hop(1)
    spread_second(away, nline - 1)
    hop_right(nline - 1, 1)
    for h in hops:
        spread_first(near, h)
    for h in hops:
        spread_third(away, h)
    load_r.wait()
    if not early:
        load_a.wait()
    core_whole(0).wait_recv()
    spread_last(away)

    def swap_copy(d, f, e):
        strips = partner(e)
        slot = order_of(d, line, nline) * CORES + f
        there = flip(line, d, nline) * CORES + flip(core, f, CORES)
        return remote(h_ref.at[d * CORES + f, :, strips], g_ref.at[slot, :, strips], swap_send.at[0],
                      swap_recv.at[slot, e], pair, there)

    def swap_arrival(s, e):
        block = g_ref.at[s, :, partner(e)]
        return remote(block, block, swap_send.at[0], swap_recv.at[s, e], pair, sibling)

    def half(d, f):
        there = flip(line, d, nline) * CORES + flip(core, f, CORES)
        start = pl.multiple_of(there * width, width)
        block = jnp.dot(a_ref[...].reshape(own * rows, cols), r_ref[:, pl.ds(start, width)],
                        preferred_element_type=jnp.float32)
        return block.astype(jnp.bfloat16).reshape(own, npair, strip, width)

    def rotate(d, first=0):
        def one(f, carry):
            h_ref[d * CORES + f] = half(d, f)
            for e in peers[::-1] + (0,):
                swap_copy(d, f, e).start()
            return carry

        lax.fori_loop(first, CORES, one, 0)

    def in_rows(s, position):
        return g_ref.at[s, :, position, pl.ds(early, late), :]

    def in_copy(s, e):
        return remote(in_rows(s, partner(e)), x_ref.at[s, pair], in_send.at[0], in_recv.at[s], partner(e), mat)

    def in_local(s):
        return pltpu.make_async_copy(in_rows(s, pair), x_ref.at[s, pair], in_recv.at[s])

    def out_rows(s, start, count):
        at = flip(core, s % CORES, CORES) * rows + pair * strip + start
        return z_ref.at[s // CORES, :, pl.ds(pl.multiple_of(at, BLOCK), count), :]

    def pass_copy(s, e):
        return remote(g_ref.at[s, :, partner(e), pl.ds(0, early), :], out_rows(s, 0, early),
                      pass_send.at[0], out_recv.at[s], partner(e), mat)

    def pass_local(s):
        return pltpu.make_async_copy(g_ref.at[s, :, pair, pl.ds(0, early), :], out_rows(s, 0, early),
                                     out_recv.at[s])

    def out_copy(s, e):
        return remote(y_ref.at[s, partner(e)], out_rows(s, early, late), out_send.at[0], out_recv.at[s],
                      partner(e), mat)

    def out_local(s):
        return pltpu.make_async_copy(y_ref.at[s, pair], out_rows(s, early, late), out_recv.at[s])

    def enter(s):
        for e in peers[::-1] + (0,):
            if s > 0:
                swap_arrival(s, e).wait_recv()
            if e:
                launch(lambda e=e: in_copy(s, e))
        in_local(s).start()
        if early:
            for e in peers[::-1]:
                launch(lambda e=e: pass_copy(s, e))
            pass_local(s).start()

    def mix(s):
        await_bytes(x_ref.at[s], in_recv.at[s])

        def chunk(b, carry):
            at = pl.ds(pl.multiple_of(b * BLOCK, BLOCK), BLOCK)
            block = x_ref[s, :, :, at, :].reshape(nsel * BLOCK, width)
            mixed = jnp.dot(kron_ref[...], block, preferred_element_type=jnp.float32)
            y_ref[s, :, :, at, :] = mixed.astype(jnp.bfloat16).reshape(npair, ntg, BLOCK, width)
            return carry

        lax.fori_loop(0, late // BLOCK, chunk, 0)
        for e in peers[::-1]:
            launch(lambda e=e: out_copy(s, e))
        out_local(s).start()

    tile = cols

    def arrived(s):
        await_bytes(z_ref.at[s // CORES, :, pl.ds(0, rows), :], out_recv.at[s])

    steps = cols // tile

    def product(i, f, add, last):
        source = flip(line, offset_of(i, line, nline), nline)
        if f is None:
            depth = pl.ds(0, CORES * rows)
        else:
            depth = pl.ds(pl.multiple_of(flip(core, f, CORES) * rows, rows), rows)

        def target(n, carry):
            t, at = n // steps, pl.ds(pl.multiple_of(n % steps * tile, tile), tile)
            part = jnp.dot(lt_ref[source, at, depth], z_ref[i, t, depth, :], preferred_element_type=jnp.float32)
            if add:
                part = part + acc_ref[t, at, :]
            if last:
                stage_ref[t, at, :] = part.astype(jnp.bfloat16)
            else:
                acc_ref[t, at, :] = part
            return carry

        return target

    def finish(i):
        for f in range(CORES):
            arrived(i * CORES + f)
        lax.fori_loop(0, ntg * steps, product(i, None, i > 0, False), 0)

    def finish_last():
        i = nline - 1
        for f in range(CORES):
            arrived(i * CORES + f)
            if f < CORES - 1:
                lax.fori_loop(0, ntg * steps, product(i, f, i + f > 0, False), 0)
        for t in range(ntg):
            lax.fori_loop(t * steps, (t + 1) * steps, product(i, CORES - 1, True, True), 0)

    for d in range(nline - 1, nline // 2 - 1, -1):
        rotate(d)
    for h in range(2, nline - 1):
        left_hop(h)
    for h in hops:
        spread_second(near, h)
    for h in range(1, nline - 1):
        left_first(h)
    for h in hops:
        spread_third(near, h)
    spread_last(near)
    g_ref[0] = half(0, 0)
    enter(0)
    rotate(0, 1)
    enter(1)
    for d in range(1, nline // 2):
        rotate(d)
    for e in peers:
        launch(lambda e=e: next_copy(e))

    for i in range(nline):
        first = i * CORES
        if i > 0:
            for f in range(CORES):
                enter(first + f)
        if i == min(3, nline - 1):
            left_beside()
        for f in range(CORES):
            mix(first + f)
            stage = i * CORES + f
            last = nline - 1
            if stage == 0:
                for h in range(1, last):
                    spread_second(LEFT, h)
                left_first(last)
            if stage == 1:
                for h in range(1, last):
                    spread_third(LEFT, h)
            if stage == 2:
                spread_second(LEFT, last)
            if stage == min(4, nmat - 1):
                spread_third(LEFT, last)
            if i > 0 and f == (CORES - 1 if i == nline - 1 else 0):
                if i == 1:
                    core_whole(LEFT).wait_recv()
                if i == min(2, nline - 1):
                    spread_last(LEFT)
                if i == min(3, nline - 1):
                    spread_last(BESIDE)
                finish(i - 1)
    finish_last()

    count = (nline - 1) * (npair - 1)
    for m in range(2):
        await_bytes(r_ref.at[pl.ds(0, count * strip), pl.ds(0, cols // 2)], plane_send.at[m])
    if nline > 2:
        await_bytes(lt_ref.at[pl.ds(0, nline - 2), pl.ds(0, (npair - 1) * mpiece), pl.ds(0, rows)],
                    plane_send.at[LEFT])
        await_bytes(gathered(LEFT), core_send.at[LEFT])
    await_bytes(lt_ref.at[0, pl.ds(0, (npair - 1) * mpiece), pl.ds(0, rows)], next_send.at[0])
    for m in (0, 1, BESIDE):
        await_bytes(gathered(m), core_send.at[m])
    for m in (0, LEFT):
        core_whole(m).wait_send()
    await_bytes(h_ref.at[pl.ds(1, nmat - 1)], swap_send.at[0])
    await_bytes(x_ref.at[:, pl.ds(0, npair - 1)], in_send.at[0])
    await_bytes(y_ref.at[:, pl.ds(0, npair - 1)], out_send.at[0])
    if early:
        await_bytes(early_ref.at[pl.ds(0, npair - 1)], first_send.at[0])
        await_bytes(g_ref.at[:, :, pl.ds(0, npair - 1), pl.ds(0, early), :], pass_send.at[0])
    for m in range(LEFT + 1):
        lanes = pl.ds(0, cols if m is LEFT else cols // 2)
        pl.when(at_end)(lambda m=m, lanes=lanes: await_bytes(r_ref.at[pl.ds(0, strip), lanes], line_send.at[m]))
        pl.when(jnp.logical_not(at_end))(
            lambda m=m, lanes=lanes: await_bytes(r_ref.at[pl.ds(0, (nline + 1) * strip), lanes], line_send.at[m]))


def shards(operators, left_rot, right_rot, integrals, pair_index, target_index):
    npair, nmat = lax.axis_size("pair"), lax.axis_size("mat")
    nline = nmat // CORES
    own, rows, cols = operators.shape
    width = cols // nmat
    strip = rows // npair
    early = early_rows(own, target_index.shape[0] // npair, strip)
    ntgt, nsel = target_index.shape[0], pair_index.shape[0]
    ntg = ntgt // npair
    bf16, f32 = jnp.bfloat16, jnp.float32
    dma = pltpu.SemaphoreType.DMA
    anywhere = pl.BlockSpec(memory_space=pl.ANY)
    return pl.pallas_call(
        functools.partial(kernel, npair, nline),
        out_shape=pltpu.VMEM((ntg, cols, width), bf16),
        in_specs=[anywhere, anywhere, anywhere, anywhere, anywhere, anywhere],
        out_specs=pl.BlockSpec(memory_space=pltpu.VMEM),
        scratch_shapes=[
            pltpu.SMEM((ntgt,), jnp.int32),
            pltpu.SMEM((nsel,), jnp.int32),
            pltpu.VMEM((own, npair, strip, cols), bf16),
            pltpu.VMEM((npair, own, BLOCK, cols), bf16),
            pltpu.VMEM((cols, cols), bf16),
            pltpu.VMEM((rows, cols), bf16),
            pltpu.VMEM((nline, cols, CORES * rows), bf16),
            pltpu.VMEM(integrals.shape, f32),
            pltpu.VMEM((ntgt, integrals.shape[1]), f32),
            pltpu.VMEM((ntgt * BLOCK, nsel * BLOCK), bf16),
            pltpu.VMEM((nmat, own, npair, strip, width), bf16),
            pltpu.VMEM((nmat, own, npair, strip, width), bf16),
            pltpu.VMEM((nmat, npair, own, strip - early, width), bf16),
            pltpu.VMEM((nmat, npair, ntg, strip - early, width), bf16),
            pltpu.VMEM((nline, ntg, CORES * rows, width), bf16),
            pltpu.VMEM((ntg, cols, width), f32),
            dma((6,)),
            dma((3,)), dma((3, nline)),
            dma((3,)), dma((3, nline, npair - 1)),
            dma((4,)), dma((4,)), dma((2,)), dma((2,)),
            dma((1,)), dma((1,)),
            dma((1,)), dma((nmat, npair)),
            dma((1,)), dma((1,)),
            dma((1,)), dma((nmat,)),
            dma((1,)), dma((1,)), dma((nmat,)),
        ],
        compiler_params=pltpu.CompilerParams(
            collective_id=0, has_side_effects=True, vmem_limit_bytes=56623104),
    )(target_index, pair_index, operators.reshape(own, npair, strip, cols), right_rot, left_rot, integrals)


def solution(mesh):
    in_specs = (P("pair", "mat", None), P("mat", None), P("mat", None), P(), P(), P())
    out_specs = P("pair", None, "mat")
    return jax.shard_map(shards, mesh=mesh, in_specs=in_specs, out_specs=out_specs, check_vma=False)
```

```python
import functools

import jax
import jax.numpy as jnp
from jax import lax
from jax.experimental import pallas as pl
from jax.experimental.pallas import tpu as pltpu
from jax.sharding import PartitionSpec as P

CORES = 2
NEAR = 2
BLOCK = 16
BESIDE = 3
LEFT = 2
UP, DOWN = 0, 1
MESH_ID = pl.DeviceIdType.MESH


def flip(index, offset, count):
    total, bit = 0, 1
    while bit < count:
        total = total + bit * ((index // bit + offset // bit) % 2)
        bit *= 2
    return total


def offset_of(i, line, nline):
    if nline == 4 and i % 2 == 1:
        inner = (line + 1) // 2 % 2
        return 3 - inner if i == 1 else 2 + inner
    return 0 if i == 0 else (nline - 1 - (i - 1) // 2 if i % 2 == 1 else i // 2)


def order_of(d, line, nline):
    if nline == 4 and d >= 2:
        return 1 + 2 * ((line + 1) // 2 % 2)
    return next(i for i in range(nline) if offset_of(i, 0, nline) == d)


def early_rows(own, ntg, strip):
    return BLOCK if own == ntg and strip > BLOCK else 0


def kernel(npair, nline, targets_hbm, pairs_hbm, a_hbm, r_hbm, l_hbm, integrals_hbm, stage_ref,
           targets_ref, pairs_ref, a_ref, early_ref, r_ref, l_ref, lt_ref, integrals_ref, rows_ref, kron_ref, h_ref, g_ref, x_ref, y_ref, z_ref,
           acc_ref,
           load_sem, line_send, line_recv, plane_send, plane_recv, core_send, core_recv, whole_send, whole_recv,
           next_send, next_recv,
           swap_send, swap_recv, first_send, first_recv, in_send, in_recv, pass_send, out_send, out_recv):
    own, _, strip, cols = a_hbm.shape
    rows = npair * strip
    ntgt, nsel = targets_hbm.shape[0], pairs_hbm.shape[0]
    ntg = ntgt // npair
    nmat = nline * CORES
    width = cols // nmat
    early = early_rows(own, ntg, strip)
    late = strip - early
    mpiece = cols // npair
    pair, mat = lax.axis_index("pair"), lax.axis_index("mat")
    line, core = mat // CORES, mat % CORES
    peers = tuple(range(1, npair))
    straight = tuple(e for e in peers if e % NEAR == 0 or e // NEAR == 0)
    far = tuple(e for e in peers if e not in straight)
    hops = range(1, nline)

    def place(i, f):
        return flip(line, offset_of(i, line, nline), nline) * CORES + flip(core, f, CORES)

    def partner(e):
        return flip(pair, e, npair)

    sibling = line * CORES + flip(core, 1, CORES)
    at_end = (line == 0) | (line == nline - 1)

    def remote(src, dst, send, recv, pair_id, mat_id):
        return pltpu.make_async_remote_copy(
            src_ref=src, dst_ref=dst, send_sem=send, recv_sem=recv,
            device_id={"pair": pair_id, "mat": mat_id}, device_id_type=MESH_ID)

    def launch(make, cond=None):
        if cond is None:
            make().start()
        else:
            pl.when(cond)(lambda: make().start())

    def await_bytes(block, sem):
        pltpu.make_async_copy(block, block, sem).wait()


    load_r = pltpu.make_async_copy(r_hbm, r_ref.at[pl.ds(pl.multiple_of(mat * rows, rows), rows), :], load_sem.at[0])
    load_l = pltpu.make_async_copy(l_hbm, l_ref, load_sem.at[1])
    load_i = pltpu.make_async_copy(integrals_hbm, integrals_ref, load_sem.at[2])
    load_a = pltpu.make_async_copy(a_hbm, a_ref, load_sem.at[3])
    load_t = pltpu.make_async_copy(targets_hbm, targets_ref, load_sem.at[4])
    load_p = pltpu.make_async_copy(pairs_hbm, pairs_ref, load_sem.at[5])
    for copy in (load_t, load_p, load_l, load_i, load_r, load_a):
        copy.start()

    barrier = pltpu.get_barrier_semaphore()

    def greet(pair_id, mat_id):
        pl.semaphore_signal(barrier, inc=1, device_id={"pair": pair_id, "mat": mat_id}, device_id_type=MESH_ID)

    for e in peers:
        greet(partner(e), mat)
    greet(pair, sibling)
    pl.when(line > 0)(lambda: greet(pair, mat - CORES))
    pl.when(line < nline - 1)(lambda: greet(pair, mat + CORES))
    above, below = 1 - (line + 1) // nline, (line + nline - 1) // nline
    pl.semaphore_wait(barrier, len(peers) + 1 + above + below)

    def piece(m, source, c, origin, part=None):
        if m is not LEFT:
            at = pl.multiple_of((source * CORES + c) * rows + origin * strip, strip)
            size = cols // 2 if part is None else cols // 4
            start = m * (cols // 2) + (0 if part is None else part * size)
            return r_ref.at[pl.ds(at, strip), pl.ds(pl.multiple_of(start, size), size)]
        lanes = pl.ds(pl.multiple_of(c * rows, rows), rows)
        at = pl.multiple_of(origin * mpiece, mpiece)
        if part is None:
            return lt_ref.at[source, pl.ds(at, mpiece), lanes]
        at = pl.multiple_of(at + part * (mpiece // 2), mpiece // 2)
        return lt_ref.at[source, pl.ds(at, mpiece // 2), lanes]

    def own_piece(m):
        if m is not LEFT:
            return r_hbm.at[pl.ds(pl.multiple_of(pair * strip, strip), strip), pl.ds(m * (cols // 2), cols // 2)]
        return piece(LEFT, line, core, pair)

    def chain_copy(m, source, way, first):
        block = piece(m, source, core, pair)
        step = 1 if way == UP else -1
        return remote(own_piece(m) if first else block, block, line_send.at[m], line_recv.at[m, source],
                      pair, (line + step) * CORES + core)

    def line_arrival(m, source):
        block = piece(m, source, core, pair)
        return remote(block, block, line_send.at[m], line_recv.at[m, source], pair, sibling)

    def plane_copy(m, source, to, origin, part=None):
        block = piece(m, source, core, partner(origin), part)
        k = to ^ origin
        return remote(block, block, plane_send.at[m], plane_recv.at[m, source, k - 1], partner(to), mat)

    def plane_arrival(m, source, e):
        block = piece(m, source, core, partner(e))
        return remote(block, block, plane_send.at[m], plane_recv.at[m, source, e - 1], partner(e), mat)

    def core_copy(m, source, e, group=None):
        block = piece(m, source, core, partner(e))
        k = m if group is None else group
        return remote(block, block, core_send.at[k], core_recv.at[k], pair, sibling)

    def core_whole(m):
        if m is not LEFT:
            src, dst = r_hbm, r_ref.at[pl.ds(pl.multiple_of(mat * rows, rows), rows), :]
        else:
            src = dst = lt_ref.at[line, :, pl.ds(pl.multiple_of(core * rows, rows), rows)]
        k = 1 if m is LEFT else 0
        return remote(src, dst, whole_send.at[k], whole_recv.at[k], pair, sibling)

    def reaches(way, h):
        if way == UP:
            return line >= h, line - h
        return line + h < nline, line + h

    def both(h, act):
        for way in (UP, DOWN):
            cond, source = reaches(way, h)
            act(way, cond, source)

    def hop(m, h, ways=(UP, DOWN)):
        for way in ways:
            cond, source = reaches(way, h)
            pl.when(cond)(lambda: line_arrival(m, source).wait_recv())
            if h + 1 < nline:
                more = line < nline - 1 if way == UP else line > 0
                launch(lambda m=m, source=source, way=way: chain_copy(m, source, way, False), cond & more)

    def left_hop(h):
        if h + 1 < nline:
            for way in (UP, DOWN):
                cond, source = reaches(way, h)
                more = cond & (line < nline - 1 if way == UP else line > 0)
                pl.when(more)(lambda: line_arrival(LEFT, source).wait_recv())
                launch(lambda source=source, way=way: chain_copy(LEFT, source, way, False), more)

    def spread_way(m, way, cond, source):
        for e in straight:
            launch(lambda e=e: plane_copy(m, source, e, 0), cond)
        launch(lambda: core_copy(m, source, 0), cond)

    def spread_first(m, h):
        both(h, lambda way, cond, source: spread_way(m, way, cond, source))

    beside = flip(line, 1, nline)

    def next_copy(e):
        block = piece(LEFT, line, core, partner(e))
        return remote(block, block, next_send.at[0], next_recv.at[0], pair, beside * CORES + core)

    def left_first(h):
        def act(way, cond, source):
            ends = cond if h + 1 == nline else cond & (line == (nline - 1 if way == UP else 0))
            pl.when(ends)(lambda: line_arrival(LEFT, source).wait_recv())
            if h == 1:
                through = cond & (line % 2 == (0 if way == UP else 1))
                launch(lambda: core_copy(LEFT, source, 0, BESIDE), cond & (line % 2 == (1 if way == UP else 0)))
            else:
                through = cond
            spread_way(LEFT, way, through, source)
        both(h, act)

    def left_beside():
        await_bytes(lt_ref.at[0, pl.ds(0, (npair - 1) * mpiece), pl.ds(0, rows)], next_recv.at[0])
        for e in peers:
            launch(lambda e=e: core_copy(LEFT, beside, e, BESIDE))

    def spread_second(m, h):
        def act(way, cond, source):
            if m is LEFT and h == 1:
                cond = cond & (line % 2 == (0 if way == UP else 1))
            for e in straight:
                pl.when(cond)(lambda e=e: plane_arrival(m, source, e).wait_recv())
                for to in straight:
                    if to ^ e in far:
                        launch(lambda e=e, to=to: plane_copy(m, source, to, e, 0 if e < NEAR else 1), cond)
                launch(lambda e=e: core_copy(m, source, e), cond)
        both(h, act)

    def spread_third(m, h):
        def act(way, cond, source):
            if m is LEFT and h == 1:
                cond = cond & (line % 2 == (0 if way == UP else 1))
            for e in far:
                pl.when(cond)(lambda e=e: plane_arrival(m, source, e).wait_recv())
                launch(lambda e=e: core_copy(m, source, e), cond)
        both(h, act)

    def gathered(m):
        if m is BESIDE:
            return lt_ref.at[0, :, pl.ds(0, rows)]
        if m is LEFT:
            return lt_ref.at[pl.ds(0, nline - 2), :, pl.ds(0, rows)]
        return r_ref.at[pl.ds(0, (nline - 1) * rows), pl.ds(0, cols // 2)]

    def spread_last(m):
        if m is not LEFT or nline > 2:
            await_bytes(gathered(m), core_recv.at[m])

    def depart(m, way):
        launch(lambda: chain_copy(m, line, way, True), line < nline - 1 if way == UP else line > 0)

    def early_source(position):
        return a_hbm.at[:, position, pl.ds(0, early), :]

    def early_copy(e):
        return remote(early_source(partner(e)), early_ref.at[pair], first_send.at[0], first_recv.at[0],
                      partner(e), mat)

    def early_mix():
        await_bytes(early_ref, first_recv.at[0])
        load_a.wait()
        span = min(512, cols)

        def columns(b, carry):
            at = pl.ds(pl.multiple_of(b * span, span), span)
            mixed = jnp.dot(kron_ref[...], early_ref[:, :, :, at].reshape(nsel * BLOCK, span),
                            preferred_element_type=jnp.float32)
            mixed = mixed.astype(jnp.bfloat16).reshape(npair, ntg, BLOCK, span)
            for position in range(npair):
                a_ref[:, position, pl.ds(0, early), at] = mixed[position]
            return carry

        lax.fori_loop(0, cols // span, columns, 0)

    for turn_of in range(2):
        depart(turn_of, UP)
        depart(1 - turn_of, DOWN)
    launch(lambda: core_whole(0))
    if early:
        for e in peers[::-1]:
            launch(lambda e=e: early_copy(e))
        pltpu.make_async_copy(early_source(pair), early_ref.at[pair], first_recv.at[0]).start()

    load_l.wait()
    lanes = pl.ds(pl.multiple_of(core * rows, rows), rows)

    def turn(b, carry):
        at = pl.ds(pl.multiple_of(b * 256, 256), 256)
        lt_ref[line, at, lanes] = l_ref[:, at].T
        return carry

    lax.fori_loop(0, cols // 256, turn, 0)

    load_i.wait()
    load_t.wait()
    load_p.wait()
    for t in range(ntgt):
        rows_ref[pl.ds(t, 1), :] = integrals_ref[pl.ds(targets_ref[t], 1), :]
    picked = rows_ref[...]
    lane = lax.broadcasted_iota(jnp.int32, picked.shape, 1)
    column = lax.broadcasted_iota(jnp.int32, (ntgt, nsel), 1)
    coupling = jnp.zeros((ntgt, nsel), jnp.float32)
    for k in range(nsel):
        value = jnp.sum(jnp.where(lane == pairs_ref[k], picked, 0.0), axis=1, keepdims=True)
        coupling = jnp.where(column == k, value, coupling)
    down = lax.broadcasted_iota(jnp.int32, (ntgt * BLOCK, ntgt), 0) // BLOCK
    tall = (down == lax.broadcasted_iota(jnp.int32, (ntgt * BLOCK, ntgt), 1)).astype(jnp.bfloat16)
    across = lax.broadcasted_iota(jnp.int32, (nsel, nsel * BLOCK), 1) // BLOCK
    broad = (across == lax.broadcasted_iota(jnp.int32, (nsel, nsel * BLOCK), 0)).astype(jnp.bfloat16)
    wide = jnp.dot(coupling.astype(jnp.bfloat16), broad, preferred_element_type=jnp.float32).astype(jnp.bfloat16)
    full = jnp.dot(tall, wide, preferred_element_type=jnp.float32)
    same = (lax.broadcasted_iota(jnp.int32, full.shape, 0) % BLOCK
            == lax.broadcasted_iota(jnp.int32, full.shape, 1) % BLOCK)
    kron_ref[...] = jnp.where(same, full, 0.0).astype(jnp.bfloat16)

    near = line // (nline // 2)
    away = 1 - near

    def hop_right(h, turn_of):
        for way, m in ((UP, turn_of), (DOWN, 1 - turn_of)):
            hop(m, h, (way,))
            cond, source = reaches(way, h)
            spread_way(m, way, cond & (away == m), source)

    for h in range(1, nline - 1):
        hop_right(h, 0)
        hop_right(h, 1)
    depart(LEFT, UP)
    depart(LEFT, DOWN)
    launch(lambda: core_whole(LEFT))
    hop_right(nline - 1, 0)
    for h in range(1, nline - 1):
        spread_second(away, h)
    left_hop(1)
    spread_second(away, nline - 1)
    hop_right(nline - 1, 1)
    for h in hops:
        spread_first(near, h)
    if early:
        early_mix()
    for h in hops:
        spread_third(away, h)
    load_r.wait()
    if not early:
        load_a.wait()
    core_whole(0).wait_recv()
    spread_last(away)

    def swap_copy(d, f, e):
        strips = partner(e)
        slot = order_of(d, line, nline) * CORES + f
        there = flip(line, d, nline) * CORES + flip(core, f, CORES)
        return remote(h_ref.at[d * CORES + f, :, strips], g_ref.at[slot, :, strips], swap_send.at[0],
                      swap_recv.at[slot, e], pair, there)

    def swap_arrival(s, e):
        block = g_ref.at[s, :, partner(e)]
        return remote(block, block, swap_send.at[0], swap_recv.at[s, e], pair, sibling)

    def half(d, f):
        there = flip(line, d, nline) * CORES + flip(core, f, CORES)
        start = pl.multiple_of(there * width, width)
        block = jnp.dot(a_ref[...].reshape(own * rows, cols), r_ref[:, pl.ds(start, width)],
                        preferred_element_type=jnp.float32)
        return block.astype(jnp.bfloat16).reshape(own, npair, strip, width)

    def rotate(d, first=0):
        def one(f, carry):
            h_ref[d * CORES + f] = half(d, f)
            for e in peers[::-1] + (0,):
                swap_copy(d, f, e).start()
            return carry

        lax.fori_loop(first, CORES, one, 0)

    def in_rows(s, position):
        return g_ref.at[s, :, position, pl.ds(early, late), :]

    def in_copy(s, e):
        return remote(in_rows(s, partner(e)), x_ref.at[s, pair], in_send.at[0], in_recv.at[s], partner(e), mat)

    def in_local(s):
        return pltpu.make_async_copy(in_rows(s, pair), x_ref.at[s, pair], in_recv.at[s])

    def out_rows(s, start, count):
        at = flip(core, s % CORES, CORES) * rows + pair * strip + start
        return z_ref.at[s // CORES, :, pl.ds(pl.multiple_of(at, BLOCK), count), :]

    def pass_copy(s, e):
        return remote(g_ref.at[s, :, partner(e), pl.ds(0, early), :], out_rows(s, 0, early),
                      pass_send.at[0], out_recv.at[s], partner(e), mat)

    def pass_local(s):
        return pltpu.make_async_copy(g_ref.at[s, :, pair, pl.ds(0, early), :], out_rows(s, 0, early),
                                     out_recv.at[s])

    def out_copy(s, e):
        return remote(y_ref.at[s, partner(e)], out_rows(s, early, late), out_send.at[0], out_recv.at[s],
                      partner(e), mat)

    def out_local(s):
        return pltpu.make_async_copy(y_ref.at[s, pair], out_rows(s, early, late), out_recv.at[s])

    def enter(s):
        for e in peers[::-1] + (0,):
            if s > 0:
                swap_arrival(s, e).wait_recv()
            if e:
                launch(lambda e=e: in_copy(s, e))
        in_local(s).start()
        if early:
            for e in peers[::-1]:
                launch(lambda e=e: pass_copy(s, e))
            pass_local(s).start()

    def mix(s):
        await_bytes(x_ref.at[s], in_recv.at[s])

        def chunk(b, carry):
            at = pl.ds(pl.multiple_of(b * BLOCK, BLOCK), BLOCK)
            block = x_ref[s, :, :, at, :].reshape(nsel * BLOCK, width)
            mixed = jnp.dot(kron_ref[...], block, preferred_element_type=jnp.float32)
            y_ref[s, :, :, at, :] = mixed.astype(jnp.bfloat16).reshape(npair, ntg, BLOCK, width)
            return carry

        lax.fori_loop(0, late // BLOCK, chunk, 0, unroll=True)
        for e in peers[::-1]:
            launch(lambda e=e: out_copy(s, e))
        out_local(s).start()

    tile = cols

    def arrived(s):
        await_bytes(z_ref.at[s // CORES, :, pl.ds(0, rows), :], out_recv.at[s])

    steps = cols // tile

    def product(i, f, add, last):
        source = flip(line, offset_of(i, line, nline), nline)
        if f is None:
            depth = pl.ds(0, CORES * rows)
        else:
            depth = pl.ds(pl.multiple_of(flip(core, f, CORES) * rows, rows), rows)

        def target(n, carry):
            t, at = n // steps, pl.ds(pl.multiple_of(n % steps * tile, tile), tile)
            part = jnp.dot(lt_ref[source, at, depth], z_ref[i, t, depth, :], preferred_element_type=jnp.float32)
            if add:
                part = part + acc_ref[t, at, :]
            if last:
                stage_ref[t, at, :] = part.astype(jnp.bfloat16)
            else:
                acc_ref[t, at, :] = part
            return carry

        return target

    def finish(i):
        for f in range(CORES):
            arrived(i * CORES + f)
        lax.fori_loop(0, ntg * steps, product(i, None, i > 0, False), 0)

    def finish_last():
        i = nline - 1
        for f in range(CORES):
            arrived(i * CORES + f)
            if f < CORES - 1:
                lax.fori_loop(0, ntg * steps, product(i, f, i + f > 0, False), 0)
        for t in range(ntg):
            lax.fori_loop(t * steps, (t + 1) * steps, product(i, CORES - 1, True, True), 0)

    for d in range(nline - 1, nline // 2 - 1, -1):
        rotate(d)
    for h in range(2, nline - 1):
        left_hop(h)
    for h in hops:
        spread_second(near, h)
    for h in range(1, nline - 1):
        left_first(h)
    for h in hops:
        spread_third(near, h)
    spread_last(near)
    g_ref[0] = half(0, 0)
    enter(0)
    rotate(0, 1)
    enter(1)
    for d in range(1, nline // 2):
        rotate(d)
    for e in peers:
        launch(lambda e=e: next_copy(e))

    for i in range(nline):
        first = i * CORES
        if i > 0:
            for f in range(CORES):
                enter(first + f)
        if i == min(3, nline - 1):
            left_beside()
        for f in range(CORES):
            mix(first + f)
            stage = i * CORES + f
            last = nline - 1
            if stage == 0:
                for h in range(1, last):
                    spread_second(LEFT, h)
                left_first(last)
            if stage == 1:
                for h in range(1, last):
                    spread_third(LEFT, h)
            if stage == 2:
                spread_second(LEFT, last)
            if stage == min(4, nmat - 1):
                spread_third(LEFT, last)
            if i > 0 and f == (CORES - 1 if i == nline - 1 else 0):
                if i == 1:
                    core_whole(LEFT).wait_recv()
                if i == min(2, nline - 1):
                    spread_last(LEFT)
                if i == min(3, nline - 1):
                    spread_last(BESIDE)
                finish(i - 1)
    finish_last()

    count = (nline - 1) * (npair - 1)
    for m in range(2):
        await_bytes(r_ref.at[pl.ds(0, count * strip), pl.ds(0, cols // 2)], plane_send.at[m])
    if nline > 2:
        await_bytes(lt_ref.at[pl.ds(0, nline - 2), pl.ds(0, (npair - 1) * mpiece), pl.ds(0, rows)],
                    plane_send.at[LEFT])
        await_bytes(gathered(LEFT), core_send.at[LEFT])
    await_bytes(lt_ref.at[0, pl.ds(0, (npair - 1) * mpiece), pl.ds(0, rows)], next_send.at[0])
    for m in (0, 1, BESIDE):
        await_bytes(gathered(m), core_send.at[m])
    for m in (0, LEFT):
        core_whole(m).wait_send()
    await_bytes(h_ref.at[pl.ds(1, nmat - 1)], swap_send.at[0])
    await_bytes(x_ref.at[:, pl.ds(0, npair - 1)], in_send.at[0])
    await_bytes(y_ref.at[:, pl.ds(0, npair - 1)], out_send.at[0])
    if early:
        await_bytes(early_ref.at[pl.ds(0, npair - 1)], first_send.at[0])
        await_bytes(g_ref.at[:, :, pl.ds(0, npair - 1), pl.ds(0, early), :], pass_send.at[0])
    for m in range(LEFT + 1):
        lanes = pl.ds(0, cols if m is LEFT else cols // 2)
        pl.when(at_end)(lambda m=m, lanes=lanes: await_bytes(r_ref.at[pl.ds(0, strip), lanes], line_send.at[m]))
        pl.when(jnp.logical_not(at_end))(
            lambda m=m, lanes=lanes: await_bytes(r_ref.at[pl.ds(0, (nline + 1) * strip), lanes], line_send.at[m]))


def shards(operators, left_rot, right_rot, integrals, pair_index, target_index):
    npair, nmat = lax.axis_size("pair"), lax.axis_size("mat")
    nline = nmat // CORES
    own, rows, cols = operators.shape
    width = cols // nmat
    strip = rows // npair
    early = early_rows(own, target_index.shape[0] // npair, strip)
    ntgt, nsel = target_index.shape[0], pair_index.shape[0]
    ntg = ntgt // npair
    bf16, f32 = jnp.bfloat16, jnp.float32
    dma = pltpu.SemaphoreType.DMA
    anywhere = pl.BlockSpec(memory_space=pl.ANY)
    return pl.pallas_call(
        functools.partial(kernel, npair, nline),
        out_shape=pltpu.VMEM((ntg, cols, width), bf16),
        in_specs=[anywhere, anywhere, anywhere, anywhere, anywhere, anywhere],
        out_specs=pl.BlockSpec(memory_space=pltpu.VMEM),
        scratch_shapes=[
            pltpu.SMEM((ntgt,), jnp.int32),
            pltpu.SMEM((nsel,), jnp.int32),
            pltpu.VMEM((own, npair, strip, cols), bf16),
            pltpu.VMEM((npair, own, BLOCK, cols), bf16),
            pltpu.VMEM((cols, cols), bf16),
            pltpu.VMEM((rows, cols), bf16),
            pltpu.VMEM((nline, cols, CORES * rows), bf16),
            pltpu.VMEM(integrals.shape, f32),
            pltpu.VMEM((ntgt, integrals.shape[1]), f32),
            pltpu.VMEM((ntgt * BLOCK, nsel * BLOCK), bf16),
            pltpu.VMEM((nmat, own, npair, strip, width), bf16),
            pltpu.VMEM((nmat, own, npair, strip, width), bf16),
            pltpu.VMEM((nmat, npair, own, strip - early, width), bf16),
            pltpu.VMEM((nmat, npair, ntg, strip - early, width), bf16),
            pltpu.VMEM((nline, ntg, CORES * rows, width), bf16),
            pltpu.VMEM((ntg, cols, width), f32),
            dma((6,)),
            dma((3,)), dma((3, nline)),
            dma((3,)), dma((3, nline, npair - 1)),
            dma((4,)), dma((4,)), dma((2,)), dma((2,)),
            dma((1,)), dma((1,)),
            dma((1,)), dma((nmat, npair)),
            dma((1,)), dma((1,)),
            dma((1,)), dma((nmat,)),
            dma((1,)), dma((1,)), dma((nmat,)),
        ],
        compiler_params=pltpu.CompilerParams(
            collective_id=0, has_side_effects=True, vmem_limit_bytes=56623104),
    )(target_index, pair_index, operators.reshape(own, npair, strip, cols), right_rot, left_rot, integrals)


def solution(mesh):
    in_specs = (P("pair", "mat", None), P("mat", None), P("mat", None), P(), P(), P())
    out_specs = P("pair", None, "mat")
    return jax.shard_map(shards, mesh=mesh, in_specs=in_specs, out_specs=out_specs, check_vma=False)
```
